32 devices in a mesh: lon: 8 (over z, x), lat: 4 (over y, core).
Axes of the slice: x: 2, y: 2, z: 4, core: 2. Of those that a mesh axis runs over, the one named last changes fastest.
Arguments:
- right_side: float32 [70, 32, 512], P(None, 'lon', 'lat'), may hold values from -12 to 12
- first_guess: float32 [70, 32, 512], P(None, 'lon', 'lat'), may hold values from -1.8 to 1.8
- cell_scale: float32 [70, 32, 512], P(None, 'lon', 'lat'), may hold values from 0.6 to 1.6
- helmholtz_term: float32 [70, 32, 512], P(None, 'lon', 'lat'), may hold values from 0.05 to 0.5
- vertical_coupling: float32 [69], replicated, may hold values from 0.5 to 4
Outputs:
- solution: float32 [70, 32, 512], P(None, 'lon', 'lat')
- residual: float32 [70, 32, 512], P(None, 'lon', 'lat')
The draws below stay inside these ranges and needn't reach their ends.
All inputs are finite; a program needn't handle non-finite values.
Results may differ from the reference program's by a relative error of at most 0.00026.
Values sent between devices are 32-bit elements; how exact they have to be, the bound alone decides.
No kernel may reach another device: no remote copies, remote signals or barrier semaphores. Data moves between devices by JAX's collectives and lax.ppermute only.
A program may use at most 64 MiB of HBM per device.

```python
import math
import jax
import jax.numpy as jnp

LEV = 70
ITERS = 2
NLON = 32
NLAT = 512


def draw_right_side(key, part):
    lon_pos = jnp.arange(NLON, dtype=jnp.float32)
    ramp_factor = 1.0 + 2.0 * lon_pos / (NLON - 1)
    rough_part = jax.random.truncated_normal(key, -4.0, 4.0, (LEV, NLON, NLAT), jnp.float32)
    return rough_part * ramp_factor[None, :, None]


def shard_levels(key, shape, split, low, top_value):
    factor_of = 1.0
    for dim, blocks in split:
        draws = jax.random.uniform(jax.random.fold_in(jax.random.fold_in(key, 6), dim), (blocks,), jnp.float32, low / len(split), top_value / len(split))
        factor_of = factor_of * jnp.repeat(jnp.exp(draws), shape[dim] // blocks).reshape((-1,) + (1,) * (len(shape) - 1 - dim))
    return factor_of


def noise(rng, dims, deviation, reach, pieces=(), kind=jnp.bfloat16):
    factor_of = shard_levels(rng, dims, pieces, -0.22, 0.18) if pieces else 1.0
    values = jax.random.normal(rng, dims, jnp.float32) * deviation * factor_of
    return jnp.minimum(jnp.maximum(values, -reach), reach).astype(kind)


def setup_inputs(seed: int = 0) -> dict:
    streams_of = jax.random.split(jax.random.key(seed), 6)
    return {
        "right_side": draw_right_side(jax.random.fold_in(streams_of[5], 71), 0),
        "first_guess": noise(streams_of[1], (LEV, NLON, NLAT), 0.3, 1.8, ((1, 8), (2, 4)), jnp.float32),
        "cell_scale": jnp.clip(jnp.exp(math.log(1.6) - 0.98082923 * jax.random.uniform(streams_of[2], (LEV, NLON, NLAT), jnp.float32) ** shard_levels(streams_of[2], (LEV, NLON, NLAT), ((1, 8), (2, 4)), -0.2, 0.2)), 0.6, 1.6),
        "helmholtz_term": jnp.clip(jnp.exp(math.log(0.5) - 2.3025851 * jax.random.uniform(streams_of[3], (LEV, NLON, NLAT), jnp.float32) ** shard_levels(streams_of[3], (LEV, NLON, NLAT), ((1, 8), (2, 4)), -0.2, 0.2)), 0.05, 0.5),
        "vertical_coupling": jnp.clip(jnp.exp(jax.random.uniform(streams_of[4], (LEV - 1,), jnp.float32, math.log(0.5), math.log(4.0))), 0.5, 4.0),
    }


def operator_apply(field, cell_scale, helmholtz_term, vertical_coupling):
    half_cycle = field.shape[1] // 2
    scaled = cell_scale * field
    east_side = jnp.roll(scaled, -1, axis=1)
    west_side = jnp.roll(scaled, 1, axis=1)
    north_edge = jnp.roll(scaled[:, :, :1], half_cycle, axis=1)
    south_edge = jnp.roll(scaled[:, :, -1:], half_cycle, axis=1)
    north_side = jnp.concatenate([north_edge, scaled[:, :, :-1]], axis=2)
    south_side = jnp.concatenate([scaled[:, :, 1:], south_edge], axis=2)
    horizontal = (4.0 + helmholtz_term) * scaled - east_side - west_side - north_side - south_side
    vert_flux = vertical_coupling[:, None, None] * (scaled[:-1] - scaled[1:])
    zero_layer = jnp.zeros_like(scaled[:1])
    vertical = jnp.concatenate([vert_flux, zero_layer], axis=0) - jnp.concatenate([zero_layer, vert_flux], axis=0)
    return cell_scale * (horizontal + vertical)


def reference(right_side, first_guess, cell_scale, helmholtz_term, vertical_coupling):
    def apply_operator(field):
        return operator_apply(field, cell_scale, helmholtz_term, vertical_coupling)

    solution = first_guess
    residual = right_side - apply_operator(first_guess)
    shadow = residual
    direction = residual
    rho_now = jnp.sum(residual * residual)
    for iteration in range(ITERS):
        image_vec = apply_operator(direction)
        alpha_step = rho_now / jnp.sum(shadow * image_vec)
        half_step = residual - alpha_step * image_vec
        second_image = apply_operator(half_step)
        omega_step = jnp.sum(second_image * half_step) / jnp.sum(second_image * second_image)
        solution = solution + alpha_step * direction + omega_step * half_step
        residual = half_step - omega_step * second_image
        if iteration + 1 < ITERS:
            rho_next = jnp.sum(shadow * half_step) - omega_step * jnp.sum(shadow * second_image)
            beta_step = (rho_next / rho_now) * (alpha_step / omega_step)
            direction = residual + beta_step * (direction - omega_step * image_vec)
            rho_now = rho_next
    return solution, residual
```

```python
import jax
import jax.numpy as jnp
from jax import lax
from jax.sharding import PartitionSpec as P

AXES = ("lon", "lat")
ITERS = 2


def swap_pairs(n_lon, n_lat):
    half = n_lon // 2

    def flat(move):
        pairs = []
        for i in range(n_lon):
            for j in range(n_lat):
                k, m = move(i, j)
                pairs.append((i * n_lat + j, k * n_lat + m))
        return pairs

    def lat_odd(i, j):
        if j == 0 or j == n_lat - 1:
            return (i + half) % n_lon, j
        return i, ((j + 1) ^ 1) - 1

    return {
        "lon_even": flat(lambda i, j: (i ^ 1, j)),
        "lon_odd": flat(lambda i, j: ((((i + 1) ^ 1) - 1) % n_lon, j)),
        "lat_even": flat(lambda i, j: (i, j ^ 1)),
        "lat_odd": flat(lat_odd),
    }


def convolve(a, b):
    out = [None] * (len(a) + len(b) - 1)
    for i, x in enumerate(a):
        for j, y in enumerate(b):
            out[i + j] = x * y if out[i + j] is None else out[i + j] + x * y
    return out


def inner(a, b, moments):
    total = None
    for k, c in enumerate(convolve(a, b)):
        term = c * moments[k]
        total = term if total is None else total + term
    return total


def add_scaled(a, scale, b):
    out = []
    for k in range(max(len(a), len(b))):
        if k >= len(b):
            out.append(a[k])
        elif k >= len(a):
            out.append(scale * b[k])
        else:
            out.append(a[k] + scale * b[k])
    return out


def krylov_coefficients(moments, shift, one):
    def times_a(a):
        return add_scaled([0.0 * one] + list(a), shift, a)

    shadow = [one]
    residual = [one]
    direction = [one]
    solution = []
    rho = moments[0]
    for iteration in range(ITERS):
        image = times_a(direction)
        alpha = rho / inner(shadow, image, moments)
        half = add_scaled(residual, -alpha, image)
        second = times_a(half)
        omega = inner(second, half, moments) / inner(second, second, moments)
        solution = add_scaled(solution, alpha, direction)
        solution = add_scaled(solution, omega, half)
        residual = add_scaled(half, -omega, second)
        if iteration + 1 < ITERS:
            rho_next = inner(shadow, half, moments) - omega * inner(shadow, second, moments)
            beta = rho_next / rho * (alpha / omega)
            direction = add_scaled(residual, beta, add_scaled(direction, -omega, image))
            rho = rho_next
    return solution, residual


def body(right_side, first_guess, cell_scale, helmholtz_term, vertical_coupling):
    n_lon, n_lat = lax.axis_size("lon"), lax.axis_size("lat")
    devices = n_lon * n_lat
    pairs = swap_pairs(n_lon, n_lat)
    lon_even = lax.axis_index("lon") % 2 == 0
    lat_even = lax.axis_index("lat") % 2 == 0
    zero = jnp.zeros((1,), jnp.float32)
    below = jnp.concatenate([vertical_coupling, zero])[:, None, None]
    above = jnp.concatenate([zero, vertical_coupling])[:, None, None]
    diagonal = (4.0 + helmholtz_term) + (below + above)

    def everywhere(row):
        spread = jnp.broadcast_to(row[None], (devices,) + row.shape)
        return jnp.sum(lax.all_to_all(spread, AXES, 0, 0, tiled=True), axis=0)

    def stencil(q, west, east, north, south):
        level = jnp.zeros_like(q[:1])
        under = jnp.concatenate([q[1:], level], axis=0)
        over = jnp.concatenate([level, q[:-1]], axis=0)
        lon_sum = jnp.concatenate([q[:, 1:], east], axis=1) + jnp.concatenate([west, q[:, :-1]], axis=1)
        lat_sum = jnp.concatenate([q[:, :, 1:], south], axis=2) + jnp.concatenate([north, q[:, :, :-1]], axis=2)
        return diagonal * q - lon_sum - lat_sum - below * under - above * over

    def apply(q):
        west, east, north, south = q[:, :1], q[:, -1:], q[:, :, :1], q[:, :, -1:]
        a = lax.ppermute(jnp.where(lon_even, east, west), AXES, pairs["lon_even"])
        b = lax.ppermute(jnp.where(lon_even, west, east), AXES, pairs["lon_odd"])
        c = lax.ppermute(jnp.where(lat_even, south, north), AXES, pairs["lat_even"])
        d = lax.ppermute(jnp.where(lat_even, north, south), AXES, pairs["lat_odd"])
        return cell_scale * stencil(
            q,
            jnp.where(lon_even, b, a),
            jnp.where(lon_even, a, b),
            jnp.where(lat_even, d, c),
            jnp.where(lat_even, c, d),
        )

    scaled_guess = cell_scale * first_guess
    rough = right_side - cell_scale * stencil(
        scaled_guess,
        jnp.zeros_like(scaled_guess[:, :1]),
        jnp.zeros_like(scaled_guess[:, :1]),
        jnp.zeros_like(scaled_guess[:, :, :1]),
        jnp.zeros_like(scaled_guess[:, :, :1]),
    )
    weight = rough * rough
    lanes = jnp.arange(128)[None]
    row = jnp.where(
        lanes == 0,
        jnp.sum(weight * (cell_scale * cell_scale) * diagonal),
        jnp.where(lanes == 1, jnp.sum(weight), 0.0),
    )
    sums = everywhere(row)[0]
    shift = jnp.where(sums[1] > 0, sums[0] / sums[1], 1.0)

    vectors = [right_side - apply(scaled_guess)]
    for _ in range(2 * ITERS):
        last = vectors[-1]
        vectors.append(apply(cell_scale * last) - shift * last)
    row = jnp.zeros((1, 128), jnp.float32)
    for k in range(4 * ITERS + 1):
        row = jnp.where(lanes == k, jnp.sum(vectors[k // 2] * vectors[k - k // 2]), row)
    sums = everywhere(row)[0]
    moments = [sums[k] for k in range(4 * ITERS + 1)]
    solution, residual = krylov_coefficients(moments, shift, jnp.float32(1.0))
    out = first_guess
    for c, v in zip(solution, vectors):
        out = out + c * v
    rest = residual[0] * vectors[0]
    for c, v in zip(residual[1:], vectors[1:]):
        rest = rest + c * v
    return out, rest


def solution(mesh):
    spec = P(None, "lon", "lat")
    return jax.shard_map(
        body, mesh=mesh, in_specs=(spec, spec, spec, spec, P()), out_specs=(spec, spec), check_vma=False
    )
```

```python
import functools

import jax
import jax.numpy as jnp
from jax import lax
from jax.experimental import pallas as pl
from jax.experimental.pallas import tpu as pltpu
from jax.sharding import PartitionSpec as P

AXES = ("lon", "lat")
ITERS = 2
LANES = 128
NEAR, FAR = 2, 3
GROUP = 8
VMEM = pl.BlockSpec(memory_space=pltpu.VMEM)
SMEM = pl.BlockSpec(memory_space=pltpu.SMEM)
FIRST = (("q", 1), ("q", 2), ("g", 1), ("g", 2), ("d", 1), ("d", 2), ("s", 1))
FIELDS = ("q", "g", "d", "s")


def swap_pairs(n_lon, n_lat):
    half = n_lon // 2

    def flat(move):
        pairs = []
        for i in range(n_lon):
            for j in range(n_lat):
                k, m = move(i, j)
                pairs.append((i * n_lat + j, k * n_lat + m))
        return pairs

    def lat_odd(i, j):
        if j == 0 or j == n_lat - 1:
            return (i + half) % n_lon, j
        return i, ((j + 1) ^ 1) - 1

    return {
        "lon_even": flat(lambda i, j: (i ^ 1, j)),
        "lon_odd": flat(lambda i, j: ((((i + 1) ^ 1) - 1) % n_lon, j)),
        "lat_even": flat(lambda i, j: (i, j ^ 1)),
        "lat_odd": flat(lat_odd),
    }


def convolve(a, b):
    out = [None] * (len(a) + len(b) - 1)
    for i, x in enumerate(a):
        for j, y in enumerate(b):
            out[i + j] = x * y if out[i + j] is None else out[i + j] + x * y
    return out


def inner(a, b, moments):
    total = None
    for k, c in enumerate(convolve(a, b)):
        term = c * moments[k]
        total = term if total is None else total + term
    return total


def add_scaled(a, scale, b):
    out = []
    for k in range(max(len(a), len(b))):
        if k >= len(b):
            out.append(a[k])
        elif k >= len(a):
            out.append(scale * b[k])
        else:
            out.append(a[k] + scale * b[k])
    return out


def krylov_coefficients(moments, shift, one):
    def times_a(a):
        return add_scaled([0.0 * one] + list(a), shift, a)

    shadow = [one]
    residual = [one]
    direction = [one]
    solution = []
    rho = moments[0]
    for iteration in range(ITERS):
        image = times_a(direction)
        alpha = rho / inner(shadow, image, moments)
        half = add_scaled(residual, -alpha, image)
        second = times_a(half)
        omega = inner(second, half, moments) / inner(second, second, moments)
        solution = add_scaled(solution, alpha, direction)
        solution = add_scaled(solution, omega, half)
        residual = add_scaled(half, -omega, second)
        if iteration + 1 < ITERS:
            rho_next = inner(shadow, half, moments) - omega * inner(shadow, second, moments)
            beta = rho_next / rho * (alpha / omega)
            direction = add_scaled(residual, beta, add_scaled(direction, -omega, image))
            rho = rho_next
    return solution, residual


def lanes_of(levels):
    return lax.broadcasted_iota(jnp.int32, (levels, LANES), 1)


def turn(value, shift):
    shift %= LANES
    return value if shift == 0 else pltpu.roll(value, shift, 1)


def plane(ref, column, columns, levels, shift=0):
    return ref.at[pl.ds((1 + shift) * columns + column, levels, stride=columns), :]


def clear_ends(ref, columns, levels):
    ref[0:columns, :] = jnp.zeros((columns, LANES), jnp.float32)
    ref[(levels + 1) * columns : (levels + 2) * columns, :] = jnp.zeros((columns, LANES), jnp.float32)


def column(ref, i, own, levels):
    return ref[pl.ds(i, levels, stride=own), :]


def shifted_rows(main, strip, lane):
    main_s, main_n = turn(main, -1), turn(main, 1)
    strip_s, strip_n = turn(strip, -1), turn(strip, 1)
    first, last = lane == 0, lane == LANES - 1
    return (
        jnp.where(last, strip_s, main_s) + jnp.where(first, strip_n, main_n),
        jnp.where(last, main_s, strip_s) + jnp.where(first, main_n, strip_n),
    )


def transformed(x, b, c, h, above, below):
    return {"q": c * x, "g": c * c, "d": (4.0 + h) + (above + below), "s": c * b}


def pack_kernel(own, levels, flags, x, b, c, h, above, below, to_a, to_b, lat_a, lat_b, *fields):
    lane = lanes_of(levels)
    group = lane // GROUP
    groups = LANES // GROUP
    lon_even, lat_even, pole = flags[0], flags[1], flags[2]
    store = dict(zip(FIELDS, fields))
    north = jnp.zeros((levels, LANES), jnp.float32)
    south = north
    for i in range(own):
        values = transformed(
            column(x, i, own, levels),
            column(b, i, own, levels),
            column(c, i, own, levels),
            column(h, i, own, levels),
            above[...],
            below[...],
        )
        for f, name in enumerate(FIELDS):
            store[name][pl.ds(i, levels, stride=own), :] = values[name]
            slot = f * own + i
            rolled = turn(values[name], GROUP * slot)
            north = jnp.where(group == slot, rolled, north)
            south = jnp.where(group == (slot - 1) % groups, rolled, south)
    for k, (name, distance) in enumerate(FIRST):
        east, west = own - distance, distance - 1
        a = jnp.where(lon_even == 1, east, west)
        to_a[k] = store[name][pl.ds(a, levels, stride=own), :]
        to_b[k] = store[name][pl.ds(east + west - a, levels, stride=own), :]
    even = jnp.full((levels, LANES), lat_even, jnp.int32) == 1
    over = jnp.full((levels, LANES), pole, jnp.int32) == 1
    lat_a[...] = jnp.where(even, south, north)
    other = jnp.where(even, north, south)
    mirror = other
    for bit in (1, 2, 4):
        mirror = jnp.where((lane & bit) != 0, turn(mirror, bit), turn(mirror, -bit))
    mirror = jnp.where(even, turn(mirror, -GROUP), turn(mirror, GROUP))
    lat_b[...] = jnp.where(over, mirror, other)


def shift_kernel(own, levels, x, b, c, h, above, below, out, q_ref):
    lane = lanes_of(levels)
    clear_ends(q_ref, own, levels)
    for i in range(own):
        plane(q_ref, i, own, levels)[...] = column(c, i, own, levels) * column(x, i, own, levels)
    weighted = jnp.zeros((levels, LANES), jnp.float32)
    total = weighted
    for i in range(own):
        q = plane(q_ref, i, own, levels)[...]
        scale = column(c, i, own, levels)
        diagonal = (4.0 + column(h, i, own, levels)) + (above[...] + below[...])
        near = jnp.where(lane == LANES - 1, 0.0, turn(q, -1)) + jnp.where(lane == 0, 0.0, turn(q, 1))
        if i > 0:
            near = near + plane(q_ref, i - 1, own, levels)[...]
        if i < own - 1:
            near = near + plane(q_ref, i + 1, own, levels)[...]
        near = near + below[...] * plane(q_ref, i, own, levels, 1)[...]
        near = near + above[...] * plane(q_ref, i, own, levels, -1)[...]
        rough = column(b, i, own, levels) - scale * (diagonal * q - near)
        weight = rough * rough
        total = total + weight
        weighted = weighted + weight * (scale * scale * diagonal)
    row_lane = lax.broadcasted_iota(jnp.int32, (1, LANES), 1)
    row = jnp.where(
        row_lane == 0,
        jnp.sum(weighted, keepdims=True),
        jnp.where(row_lane == 1, jnp.sum(total, keepdims=True), 0.0),
    )
    out[...] = jnp.broadcast_to(row[None], out.shape)


def lane_value(row, k):
    lane = lax.broadcasted_iota(jnp.int32, (1, LANES), 1)
    return jnp.sum(jnp.where(lane == k, row, 0.0), axis=1, keepdims=True)


def total_row(gathered):
    return jnp.sum(gathered[...], axis=0)


class Extended:
    def __init__(self, columns, levels, d, g, above, below, lane):
        self.columns, self.levels = columns, levels
        self.d, self.g = d, g
        self.above, self.below, self.lane = above, below, lane

    def at(self, pair, k, e, shift=0):
        return plane(pair[k], e, self.columns, self.levels, shift)[...]

    def put(self, pair, k, e, value):
        plane(pair[k], e, self.columns, self.levels)[...] = value

    def stencil(self, pair, e, strips=True):
        main, strip = self.at(pair, 0, e), self.at(pair, 1, e)
        near = shifted_rows(main, strip, self.lane)
        out = []
        for k, q in enumerate((main, strip) if strips else (main,)):
            side = self.at(pair, k, e - 1) + self.at(pair, k, e + 1)
            levels = self.below[...] * self.at(pair, k, e, 1) + self.above[...] * self.at(pair, k, e, -1)
            out.append((q, self.at(self.d, k, e) * q - (side + near[k]) - levels))
        return out


def first_kernel(own, levels, columns, flags, fq, fg, fd, fs, above, below, from_a, from_b, lat_a, lat_b,
                 strips_a, strips_b, sums, k0, k1, k1_strip, to_a, to_b, g_main, g_strip, d_main, d_strip,
                 shift_out, qa_main, qa_strip, qb_main, qb_strip, s_main, s_strip):
    lane = lanes_of(levels)
    low = lane < LANES // 2
    lon_even, lat_even = flags[0], flags[1]
    even = jnp.full((levels, LANES), lat_even, jnp.int32) == 1
    qa, qb = (qa_main, qa_strip), (qb_main, qb_strip)
    where_to = {"q": qa, "g": (g_main, g_strip), "d": (d_main, d_strip), "s": (s_main, s_strip)}
    ext = Extended(columns, levels, where_to["d"], where_to["g"], above, below, lane)
    for ref in (*qa, *qb):
        clear_ends(ref, columns, levels)

    row = total_row(sums)
    weighted, total = lane_value(row, 0), lane_value(row, 1)
    shift = jnp.where(total > 0.0, weighted / jnp.where(total > 0.0, total, 1.0), 1.0)
    shift_out[...] = jnp.broadcast_to(shift, shift_out.shape)
    shift = jnp.broadcast_to(shift, (levels, LANES))

    def unpack(north, south, name, i):
        slot = FIELDS.index(name) * own + i
        back = -GROUP * slot
        return jnp.where(low, turn(south, back), turn(north, back))

    def halves(a, b):
        return jnp.where(even, b, a), jnp.where(even, a, b)

    fields = dict(zip(FIELDS, (fq, fg, fd, fs)))
    north, south = halves(lat_a[...], lat_b[...])
    for name in FIELDS:
        for i in range(own):
            ext.put(where_to[name], 0, FAR + i, column(fields[name], i, own, levels))
            ext.put(where_to[name], 1, FAR + i, unpack(north, south, name, i))
    for block, tiles, east in ((from_a, strips_a, lon_even), (from_b, strips_b, 1 - lon_even)):
        north, south = halves(tiles[0], tiles[1])
        is_east = jnp.full((levels, LANES), east, jnp.int32) == 1
        for k, (name, distance) in enumerate(FIRST):
            e_east, e_west = FAR + own - 1 + distance, FAR - distance
            e = jnp.where(east == 1, e_east, e_west)
            ext.put(where_to[name], 0, e, block[k])
            strip = jnp.where(
                is_east,
                unpack(north, south, name, distance - 1),
                unpack(north, south, name, own - distance),
            )
            ext.put(where_to[name], 1, e, strip)
    for e in range(FAR - 1, FAR + own + 1):
        for k, (_, image) in enumerate(ext.stencil(qa, e)):
            value = ext.at(where_to["s"], k, e) - ext.at(where_to["g"], k, e) * image
            ext.put(qb, k, e, value)
            if k == 0 and FAR <= e < FAR + own:
                k0[pl.ds(e - FAR, levels, stride=own), :] = value
    for e in range(FAR, FAR + own):
        for k, (q, image) in enumerate(ext.stencil(qb, e)):
            value = ext.at(where_to["g"], k, e) * image - shift * q
            out = k1 if k == 0 else k1_strip
            out[pl.ds(e - FAR, levels, stride=own), :] = value
    for out, side in ((to_a, lon_even), (to_b, 1 - lon_even)):
        packed = jnp.zeros((levels, LANES), jnp.float32)
        for distance in range(1, FAR + 1):
            i = jnp.where(side == 1, own - distance, distance - 1)
            out[distance - 1] = k1[pl.ds(i, levels, stride=own), :]
            offset = 2 * GROUP * (distance - 1) + GROUP
            rolled = turn(k1_strip[pl.ds(i, levels, stride=own), :], offset)
            packed = jnp.where(lane // (2 * GROUP) == distance - 1, rolled, packed)
        out[FAR] = packed


def second_kernel(own, levels, columns, flags, k0, k1, k1_strip, from_a, from_b, g_main, g_strip, d_main, d_strip,
                  above, below, shift_row, k2, k3, k4, out, qa_main, qa_strip, qb_main, qb_strip):
    lane = lanes_of(levels)
    lon_even = flags[0]
    qa, qb = (qa_main, qa_strip), (qb_main, qb_strip)
    g = (g_main, g_strip)
    ext = Extended(columns, levels, (d_main, d_strip), g, above, below, lane)
    for ref in (*qa, *qb):
        clear_ends(ref, columns, levels)
    shift = jnp.broadcast_to(shift_row[...], (levels, LANES))
    for i in range(own):
        ext.put(qa, 0, FAR + i, column(k1, i, own, levels))
        ext.put(qa, 1, FAR + i, column(k1_strip, i, own, levels))
    for block, east in ((from_a, lon_even), (from_b, 1 - lon_even)):
        for distance in range(1, FAR + 1):
            e = jnp.where(east == 1, FAR + own - 1 + distance, FAR - distance)
            ext.put(qa, 0, e, block[distance - 1])
            ext.put(qa, 1, e, turn(block[FAR], -(2 * GROUP * (distance - 1) + GROUP)))
    source, target = qa, qb
    for step, reach in ((0, FAR - 1), (1, FAR - 2)):
        for e in range(FAR - reach, FAR + own + reach):
            for k, (q, image) in enumerate(ext.stencil(source, e)):
                value = ext.at(g, k, e) * image - shift * q
                ext.put(target, k, e, value)
                if k == 0 and FAR <= e < FAR + own:
                    (k2, k3)[step][pl.ds(e - FAR, levels, stride=own), :] = value
        source, target = target, source
    count = 4 * ITERS + 1
    sums = [jnp.zeros((levels, LANES), jnp.float32) for _ in range(count)]
    for i in range(own):
        e = FAR + i
        ((q, image),) = ext.stencil(source, e, strips=False)
        scale = ext.at(g, 0, e)
        last = scale * image - shift * q
        k4[pl.ds(i, levels, stride=own), :] = last
        v = [column(k0, i, own, levels), column(k1, i, own, levels), column(k2, i, own, levels), q, last]
        w = 1.0 / scale
        for k in range(count):
            if k % 2 == 0:
                lead = v[k // 2] * w
            sums[k] = sums[k] + lead * v[k - k // 2]
    row_lane = lax.broadcasted_iota(jnp.int32, (1, LANES), 1)
    row = jnp.zeros((1, LANES), jnp.float32)
    for k in range(count):
        row = jnp.where(row_lane == k, jnp.sum(sums[k], keepdims=True), row)
    out[...] = jnp.broadcast_to(row[None], out.shape)


def final_kernel(sums, shift_row, x, c, k0, k1, k2, k3, k4, out, rest):
    row = total_row(sums)
    moments = [lane_value(row, k) for k in range(4 * ITERS + 1)]
    shift = lane_value(shift_row[...], 0)
    solution, residual = krylov_coefficients(moments, shift, jnp.ones((1, 1), jnp.float32))
    vectors = (k0, k1, k2, k3, k4)
    inverse = 1.0 / c[...]

    def combined(coefficients):
        total = None
        for a, v in zip(coefficients, vectors):
            term = a * v[...]
            total = term if total is None else total + term
        return total * inverse

    out[...] = x[...] + combined(solution)
    rest[...] = combined(residual)


def body(right_side, first_guess, cell_scale, helmholtz_term, vertical_coupling):
    n_lon, n_lat = lax.axis_size("lon"), lax.axis_size("lat")
    levels, own, width = right_side.shape
    assert width == LANES and own >= FAR and len(FIELDS) * own * GROUP <= LANES
    assert n_lon % 4 == 0 and n_lat % 2 == 0
    columns = own + 2 * FAR
    pairs = swap_pairs(n_lon, n_lat)
    i, j = lax.axis_index("lon"), lax.axis_index("lat")
    flags = jnp.stack([1 - i % 2, 1 - j % 2, ((j == 0) | (j == n_lat - 1)).astype(jnp.int32)]).astype(jnp.int32)
    zero = jnp.zeros((1,), jnp.float32)
    below = jnp.broadcast_to(jnp.concatenate([vertical_coupling, zero])[:, None], (levels, LANES))
    above = jnp.broadcast_to(jnp.concatenate([zero, vertical_coupling])[:, None], (levels, LANES))
    b, x, c, h = (v.reshape(levels * own, LANES) for v in (right_side, first_guess, cell_scale, helmholtz_term))

    def real(*shape):
        return jax.ShapeDtypeStruct(shape, jnp.float32)

    def call(kernel, ins, outs, scratch=(), flagged=True):
        return pl.pallas_call(
            kernel,
            out_shape=tuple(outs) if len(outs) > 1 else outs[0],
            in_specs=[SMEM] * flagged + [VMEM] * (len(ins) - flagged),
            out_specs=tuple([VMEM] * len(outs)) if len(outs) > 1 else VMEM,
            scratch_shapes=[pltpu.VMEM(s, jnp.float32) for s in scratch],
            compiler_params=pltpu.CompilerParams(vmem_limit_bytes=32 * 1024 * 1024),
        )(*ins)

    def swap(value, name):
        return lax.ppermute(value, AXES, pairs[name])

    def everywhere(rows):
        return lax.all_to_all(rows, AXES, 0, 0, tiled=True)

    whole = real(levels * own, LANES)
    tile = real(levels, LANES)
    rows = real(n_lon * n_lat, 1, LANES)
    padded = ((levels + 2) * own, LANES)
    extended = ((levels + 2) * columns, LANES)

    to_a, to_b, lat_a, lat_b, *fields = call(
        functools.partial(pack_kernel, own, levels),
        (flags, x, b, c, h, above, below),
        [real(len(FIRST), levels, LANES)] * 2 + [tile] * 2 + [whole] * len(FIELDS),
    )
    from_a, from_b = swap(to_a, "lon_even"), swap(to_b, "lon_odd")
    lat_a, lat_b = swap(lat_a, "lat_even"), swap(lat_b, "lat_odd")
    strips = jnp.stack([lat_a, lat_b])
    strips_a, strips_b = swap(strips, "lon_even"), swap(strips, "lon_odd")
    weights = call(
        functools.partial(shift_kernel, own, levels), (x, b, c, h, above, below), [rows], [padded], flagged=False
    )
    weights = everywhere(weights)
    k0, k1, k1_strip, to_a, to_b, *coefficients, shift = call(
        functools.partial(first_kernel, own, levels, columns),
        (flags, *fields, above, below, from_a, from_b, lat_a, lat_b, strips_a, strips_b, weights),
        [whole] * 3 + [real(FAR + 1, levels, LANES)] * 2 + [real(*extended)] * 4 + [real(1, LANES)],
        [extended] * 6,
    )
    from_a, from_b = swap(to_a, "lon_even"), swap(to_b, "lon_odd")
    k2, k3, k4, sums = call(
        functools.partial(second_kernel, own, levels, columns),
        (flags, k0, k1, k1_strip, from_a, from_b, *coefficients, above, below, shift),
        [whole] * 3 + [rows],
        [extended] * 4,
    )
    sums = everywhere(sums)
    out, rest = call(final_kernel, (sums, shift, x, c, k0, k1, k2, k3, k4), [whole] * 2, flagged=False)
    return out.reshape(right_side.shape), rest.reshape(right_side.shape)


def solution(mesh):
    spec = P(None, "lon", "lat")
    return jax.shard_map(
        body, mesh=mesh, in_specs=(spec, spec, spec, spec, P()), out_specs=(spec, spec), check_vma=False
    )
```

```python
import functools

import jax
import jax.numpy as jnp
from jax import lax
from jax.experimental import pallas as pl
from jax.experimental.pallas import tpu as pltpu
from jax.sharding import PartitionSpec as P


AXES = ("lon", "lat")
ITERS = 2
LANES = 128
NEAR, FAR = 2, 3
GROUP = 8
VMEM = pl.BlockSpec(memory_space=pltpu.VMEM)
FIRST = (("q", 1), ("q", 2), ("g", 1), ("g", 2), ("d", 1), ("d", 2), ("s", 1))
FIELDS = ("q", "g", "d", "s")


def swap_pairs(n_lon, n_lat):
    half = n_lon // 2

    def flat(move):
        pairs = []
        for i in range(n_lon):
            for j in range(n_lat):
                k, m = move(i, j)
                pairs.append((i * n_lat + j, k * n_lat + m))
        return pairs

    def lat_odd(i, j):
        if j == 0 or j == n_lat - 1:
            return (i + half) % n_lon, j
        return i, ((j + 1) ^ 1) - 1

    return {
        "lon_even": flat(lambda i, j: (i ^ 1, j)),
        "lon_odd": flat(lambda i, j: ((((i + 1) ^ 1) - 1) % n_lon, j)),
        "lat_even": flat(lambda i, j: (i, j ^ 1)),
        "lat_odd": flat(lat_odd),
    }


def convolve(a, b):
    out = [None] * (len(a) + len(b) - 1)
    for i, x in enumerate(a):
        for j, y in enumerate(b):
            out[i + j] = x * y if out[i + j] is None else out[i + j] + x * y
    return out


def inner(a, b, moments):
    total = None
    for k, c in enumerate(convolve(a, b)):
        term = c * moments[k]
        total = term if total is None else total + term
    return total


def add_scaled(a, scale, b):
    out = []
    for k in range(max(len(a), len(b))):
        if k >= len(b):
            out.append(a[k])
        elif k >= len(a):
            out.append(scale * b[k])
        else:
            out.append(a[k] + scale * b[k])
    return out


def krylov_coefficients(moments, shift, one):
    def times_a(a):
        return add_scaled([0.0 * one] + list(a), shift, a)

    shadow = [one]
    residual = [one]
    direction = [one]
    solution = []
    rho = moments[0]
    for iteration in range(ITERS):
        image = times_a(direction)
        alpha = rho / inner(shadow, image, moments)
        half = add_scaled(residual, -alpha, image)
        second = times_a(half)
        omega = inner(second, half, moments) / inner(second, second, moments)
        solution = add_scaled(solution, alpha, direction)
        solution = add_scaled(solution, omega, half)
        residual = add_scaled(half, -omega, second)
        if iteration + 1 < ITERS:
            rho_next = inner(shadow, half, moments) - omega * inner(shadow, second, moments)
            beta = rho_next / rho * (alpha / omega)
            direction = add_scaled(residual, beta, add_scaled(direction, -omega, image))
            rho = rho_next
    return solution, residual


def lanes_of(levels):
    return lax.broadcasted_iota(jnp.int32, (levels, LANES), 1)


def turn(value, shift):
    shift %= LANES
    return value if shift == 0 else pltpu.roll(value, shift, 1)


def plane(ref, column, columns, levels, shift=0):
    return ref.at[pl.ds((1 + shift) * columns + column, levels, stride=columns), :]


def clear_ends(ref, columns, levels):
    ref[0:columns, :] = jnp.zeros((columns, LANES), jnp.float32)
    ref[(levels + 1) * columns : (levels + 2) * columns, :] = jnp.zeros((columns, LANES), jnp.float32)


def column(ref, i, own, levels):
    return ref[pl.ds(i, levels, stride=own), :]


def shifted_rows(main, strip, lane):
    main_s, main_n = turn(main, -1), turn(main, 1)
    strip_s, strip_n = turn(strip, -1), turn(strip, 1)
    first, last = lane == 0, lane == LANES - 1
    return (
        jnp.where(last, strip_s, main_s) + jnp.where(first, strip_n, main_n),
        jnp.where(last, main_s, strip_s) + jnp.where(first, main_n, strip_n),
    )


def transformed(x, b, c, h, above, below):
    return {"q": c * x, "g": c * c, "d": (4.0 + h) + (above + below), "s": c * b}


def parity(size):
    i, j = lax.axis_index("lon"), lax.axis_index("lat")
    pole = (j == 0) | (j == size - 1)
    return 1 - lax.rem(i, 2), 1 - lax.rem(j, 2), pole


def shift_sums(own, levels, fq, fg, fd, fs, above, below, out, q_ref):
    lane = lanes_of(levels)
    clear_ends(q_ref, own, levels)
    q_ref[own : own * (levels + 1), :] = fq[...]
    weighted = jnp.zeros((levels, LANES), jnp.float32)
    total = weighted
    for i in range(own):
        q = plane(q_ref, i, own, levels)[...]
        scale = column(fg, i, own, levels)
        diagonal = column(fd, i, own, levels)
        near = jnp.where(lane == LANES - 1, 0.0, turn(q, -1)) + jnp.where(lane == 0, 0.0, turn(q, 1))
        if i > 0:
            near = near + plane(q_ref, i - 1, own, levels)[...]
        if i < own - 1:
            near = near + plane(q_ref, i + 1, own, levels)[...]
        near = near + below[...] * plane(q_ref, i, own, levels, 1)[...]
        near = near + above[...] * plane(q_ref, i, own, levels, -1)[...]
        rough = column(fs, i, own, levels) - scale * (diagonal * q - near)
        square = rough * rough
        total = total + square / scale
        weighted = weighted + square * diagonal
    row_lane = lax.broadcasted_iota(jnp.int32, (1, LANES), 1)
    row = jnp.where(
        row_lane == 0,
        jnp.sum(weighted, keepdims=True),
        jnp.where(row_lane == 1, jnp.sum(total, keepdims=True), 0.0),
    )
    out[...] = jnp.broadcast_to(row[None], out.shape)


def pack_kernel(own, levels, n_lat, x_hbm, b_hbm, c_hbm, h_hbm, coupling_hbm, to_a, to_b, lat_a, lat_b, above,
                below, fq, fg, fd, fs, weights, x, b, c, h, coupling, q_ref, sem):
    copies = []
    moves = ((coupling_hbm, coupling), (x_hbm, x), (c_hbm, c), (h_hbm, h), (b_hbm, b))
    for k, (source, target) in enumerate(moves):
        copies.append(pltpu.make_async_copy(source, target, sem.at[k]))
        copies[-1].start()
    lane = lanes_of(levels)
    group = lane // GROUP
    groups = LANES // GROUP
    lon_even, lat_even, pole = parity(n_lat)
    store = dict(zip(FIELDS, (fq, fg, fd, fs)))
    copies[0].wait()
    wide = (levels, levels - 1)
    row, interface = (lax.broadcasted_iota(jnp.int32, wide, k) for k in (0, 1))
    strength = jnp.broadcast_to(coupling[...], wide)
    for out, k in ((below, row), (above, row - 1)):
        value = jnp.sum(jnp.where(interface == k, strength, 0.0), axis=1, keepdims=True)
        out[...] = jnp.broadcast_to(value, (levels, LANES))
    north = jnp.zeros((levels, LANES), jnp.float32)
    south = north
    for copy in copies[1:]:
        copy.wait()
    for i in range(own):
        values = transformed(
            column(x, i, own, levels),
            column(b, i, own, levels),
            column(c, i, own, levels),
            column(h, i, own, levels),
            above[...],
            below[...],
        )
        for f, name in enumerate(FIELDS):
            store[name][pl.ds(i, levels, stride=own), :] = values[name]
            slot = f * own + i
            rolled = turn(values[name], GROUP * slot)
            north = jnp.where(group == slot, rolled, north)
            south = jnp.where(group == (slot - 1) % groups, rolled, south)
    even = jnp.full((levels, LANES), lat_even, jnp.int32) == 1
    over = jnp.full((levels, LANES), pole.astype(jnp.int32), jnp.int32) == 1
    lat_a[...] = jnp.where(even, south, north)
    other = jnp.where(even, north, south)
    mirror = other
    for bit in (1, 2, 4):
        mirror = jnp.where((lane & bit) != 0, turn(mirror, bit), turn(mirror, -bit))
    mirror = jnp.where(even, turn(mirror, -GROUP), turn(mirror, GROUP))
    lat_b[...] = jnp.where(over, mirror, other)
    for k, (name, distance) in enumerate(FIRST):
        east, west = own - distance, distance - 1
        a = jnp.where(lon_even == 1, east, west)
        to_a[k] = store[name][pl.ds(a, levels, stride=own), :]
        to_b[k] = store[name][pl.ds(east + west - a, levels, stride=own), :]
    shift_sums(own, levels, fq, fg, fd, fs, above, below, weights, q_ref)


def corner_kernel(own, levels, n_lat, lat_a, lat_b, to_a, to_b):
    lane = lanes_of(levels)
    quarter = (lane // GROUP) % own
    lon_even, lat_even, _ = parity(n_lat)
    even = jnp.full((levels, LANES), lat_even, jnp.int32) == 1
    lon = jnp.full((levels, LANES), lon_even, jnp.int32) == 1
    a, b = lat_a[...], lat_b[...]
    north, south = jnp.where(even, b, a), jnp.where(even, a, b)
    east = jnp.where(quarter >= own - NEAR, south, turn(north, GROUP * (1 - NEAR)))
    west = jnp.where(quarter < NEAR, south, turn(north, GROUP * (1 + NEAR)))
    to_a[...] = jnp.where(lon, east, west)
    to_b[...] = jnp.where(lon, west, east)


def lane_value(row, k):
    lane = lax.broadcasted_iota(jnp.int32, (1, LANES), 1)
    return jnp.sum(jnp.where(lane == k, row, 0.0), axis=1, keepdims=True)


def total_row(gathered):
    return jnp.sum(gathered[...], axis=0)


class Extended:
    def __init__(self, columns, levels, d, g, above, below, lane):
        self.columns, self.levels = columns, levels
        self.d, self.g = d, g
        self.above, self.below, self.lane = above, below, lane

    def at(self, pair, k, e, shift=0):
        return plane(pair[k], e, self.columns, self.levels, shift)[...]

    def put(self, pair, k, e, value):
        plane(pair[k], e, self.columns, self.levels)[...] = value

    def stencil(self, pair, e, strips=True):
        main, strip = self.at(pair, 0, e), self.at(pair, 1, e)
        near = shifted_rows(main, strip, self.lane)
        out = []
        for k, q in enumerate((main, strip) if strips else (main,)):
            side = self.at(pair, k, e - 1) + self.at(pair, k, e + 1)
            levels = self.below[...] * self.at(pair, k, e, 1) + self.above[...] * self.at(pair, k, e, -1)
            out.append((q, self.at(self.d, k, e) * q - (side + near[k]) - levels))
        return out


def first_kernel(own, levels, columns, n_lat, fq, fg, fd, fs, above, below, from_a, from_b, lat_a, lat_b,
                 corners_a, corners_b, sums, k0, k1, k1_strip, to_a, to_b, g_main, g_strip, d_main, d_strip,
                 shift_out, qa_main, qa_strip, qb_main, qb_strip, s_main, s_strip):
    lane = lanes_of(levels)
    low = lane < LANES // 2
    lon_even, lat_even, _ = parity(n_lat)
    even = jnp.full((levels, LANES), lat_even, jnp.int32) == 1
    qa, qb = (qa_main, qa_strip), (qb_main, qb_strip)
    where_to = {"q": qa, "g": (g_main, g_strip), "d": (d_main, d_strip), "s": (s_main, s_strip)}
    ext = Extended(columns, levels, where_to["d"], where_to["g"], above, below, lane)
    for ref in (*qa, *qb):
        clear_ends(ref, columns, levels)

    row = total_row(sums)
    weighted, total = lane_value(row, 0), lane_value(row, 1)
    shift = jnp.where(total > 0.0, weighted / jnp.where(total > 0.0, total, 1.0), 1.0)
    shift_out[...] = jnp.broadcast_to(shift, shift_out.shape)
    shift = jnp.broadcast_to(shift, (levels, LANES))

    def unpack(north, south, name, i):
        back = -GROUP * (FIELDS.index(name) * own + i)
        return jnp.where(low, turn(south, back), turn(north, back))

    fields = dict(zip(FIELDS, (fq, fg, fd, fs)))
    a, b = lat_a[...], lat_b[...]
    north, south = jnp.where(even, b, a), jnp.where(even, a, b)
    for name in FIELDS:
        for i in range(own):
            ext.put(where_to[name], 0, FAR + i, column(fields[name], i, own, levels))
            ext.put(where_to[name], 1, FAR + i, unpack(north, south, name, i))
    for block, corner, east in ((from_a, corners_a, lon_even), (from_b, corners_b, 1 - lon_even)):
        is_east = jnp.full((levels, LANES), east, jnp.int32) == 1
        tile = corner[...]
        north = jnp.where(is_east, turn(tile, -GROUP * (1 + NEAR)), turn(tile, -GROUP * (1 - NEAR)))
        for k, (name, distance) in enumerate(FIRST):
            e = jnp.where(east == 1, FAR + own - 1 + distance, FAR - distance)
            ext.put(where_to[name], 0, e, block[k])
            strip = jnp.where(
                is_east, unpack(north, tile, name, distance - 1), unpack(north, tile, name, own - distance)
            )
            ext.put(where_to[name], 1, e, strip)
    for e in range(FAR - 1, FAR + own + 1):
        for k, (_, image) in enumerate(ext.stencil(qa, e)):
            value = ext.at(where_to["s"], k, e) - ext.at(where_to["g"], k, e) * image
            ext.put(qb, k, e, value)
            if k == 0 and FAR <= e < FAR + own:
                k0[pl.ds(e - FAR, levels, stride=own), :] = value
    for e in range(FAR, FAR + own):
        for k, (q, image) in enumerate(ext.stencil(qb, e)):
            value = ext.at(where_to["g"], k, e) * image - shift * q
            out = k1 if k == 0 else k1_strip
            out[pl.ds(e - FAR, levels, stride=own), :] = value
    for out, side in ((to_a, lon_even), (to_b, 1 - lon_even)):
        packed = jnp.zeros((levels, LANES), jnp.float32)
        for distance in range(1, FAR + 1):
            i = jnp.where(side == 1, own - distance, distance - 1)
            out[distance - 1] = k1[pl.ds(i, levels, stride=own), :]
            offset = 2 * GROUP * (distance - 1) + GROUP
            rolled = turn(k1_strip[pl.ds(i, levels, stride=own), :], offset)
            packed = jnp.where(lane // (2 * GROUP) == distance - 1, rolled, packed)
        out[FAR] = packed


def second_kernel(own, levels, columns, n_lat, k0, k1, k1_strip, from_a, from_b, g_main, g_strip, d_main, d_strip,
                  above, below, shift_row, k2, k3, k4, out, qa_main, qa_strip, qb_main, qb_strip):
    lane = lanes_of(levels)
    lon_even, _, _ = parity(n_lat)
    qa, qb = (qa_main, qa_strip), (qb_main, qb_strip)
    g = (g_main, g_strip)
    ext = Extended(columns, levels, (d_main, d_strip), g, above, below, lane)
    for ref in (*qa, *qb):
        clear_ends(ref, columns, levels)
    shift = jnp.broadcast_to(shift_row[...], (levels, LANES))
    for i in range(own):
        ext.put(qa, 0, FAR + i, column(k1, i, own, levels))
        ext.put(qa, 1, FAR + i, column(k1_strip, i, own, levels))
    for block, east in ((from_a, lon_even), (from_b, 1 - lon_even)):
        for distance in range(1, FAR + 1):
            e = jnp.where(east == 1, FAR + own - 1 + distance, FAR - distance)
            ext.put(qa, 0, e, block[distance - 1])
            ext.put(qa, 1, e, turn(block[FAR], -(2 * GROUP * (distance - 1) + GROUP)))
    source, target = qa, qb
    for step, reach in ((0, FAR - 1), (1, FAR - 2)):
        for e in range(FAR - reach, FAR + own + reach):
            for k, (q, image) in enumerate(ext.stencil(source, e)):
                value = ext.at(g, k, e) * image - shift * q
                ext.put(target, k, e, value)
                if k == 0 and FAR <= e < FAR + own:
                    (k2, k3)[step][pl.ds(e - FAR, levels, stride=own), :] = value
        source, target = target, source
    count = 4 * ITERS + 1
    sums = [jnp.zeros((levels, LANES), jnp.float32) for _ in range(count)]
    for i in range(own):
        e = FAR + i
        ((q, image),) = ext.stencil(source, e, strips=False)
        scale = ext.at(g, 0, e)
        last = scale * image - shift * q
        k4[pl.ds(i, levels, stride=own), :] = last
        v = [column(k0, i, own, levels), column(k1, i, own, levels), column(k2, i, own, levels), q, last]
        w = 1.0 / scale
        for k in range(count):
            if k % 2 == 0:
                lead = v[k // 2] * w
            sums[k] = sums[k] + lead * v[k - k // 2]
    row_lane = lax.broadcasted_iota(jnp.int32, (1, LANES), 1)
    row = jnp.zeros((1, LANES), jnp.float32)
    for k in range(count):
        row = jnp.where(row_lane == k, jnp.sum(sums[k], keepdims=True), row)
    out[...] = jnp.broadcast_to(row[None], out.shape)


def final_kernel(sums, shift_row, x, c, k0, k1, k2, k3, k4, out, rest):
    row = total_row(sums)
    moments = [lane_value(row, k) for k in range(4 * ITERS + 1)]
    shift = lane_value(shift_row[...], 0)
    solution, residual = krylov_coefficients(moments, shift, jnp.ones((1, 1), jnp.float32))
    vectors = (k0, k1, k2, k3, k4)
    inverse = 1.0 / c[...]

    def combined(coefficients):
        total = None
        for a, v in zip(coefficients, vectors):
            term = a * v[...]
            total = term if total is None else total + term
        return total * inverse

    out[...] = x[...] + combined(solution)
    rest[...] = combined(residual)


def program(right_side, first_guess, cell_scale, helmholtz_term, vertical_coupling):
    n_lon, n_lat = lax.axis_size("lon"), lax.axis_size("lat")
    levels, own, width = right_side.shape
    assert width == LANES and own == 2 * NEAR >= FAR and len(FIELDS) * own * GROUP == LANES
    assert n_lon % 4 == 0 and n_lat % 2 == 0
    columns = own + 2 * FAR
    pairs = swap_pairs(n_lon, n_lat)
    coupling = vertical_coupling.reshape(1, levels - 1)
    b, x, c, h = (v.reshape(levels * own, LANES) for v in (right_side, first_guess, cell_scale, helmholtz_term))

    def real(*shape):
        return jax.ShapeDtypeStruct(shape, jnp.float32)

    def call(kernel, ins, outs, scratch=(), specs=None, grant=32 * 1024 * 1024):
        return pl.pallas_call(
            kernel,
            out_shape=tuple(outs) if len(outs) > 1 else outs[0],
            in_specs=specs or [VMEM] * len(ins),
            out_specs=tuple([VMEM] * len(outs)) if len(outs) > 1 else VMEM,
            scratch_shapes=[pltpu.VMEM(s, jnp.float32) if isinstance(s, tuple) else s for s in scratch],
            compiler_params=pltpu.CompilerParams(vmem_limit_bytes=grant),
        )(*ins)

    def swap(value, name):
        return lax.ppermute(value, AXES, pairs[name])

    def everywhere(rows):
        return lax.all_to_all(rows, AXES, 0, 0, tiled=True)

    whole = real(levels * own, LANES)
    tile = real(levels, LANES)
    rows = real(n_lon * n_lat, 1, LANES)
    padded = ((levels + 2) * own, LANES)
    extended = ((levels + 2) * columns, LANES)

    to_a, to_b, lat_a, lat_b, above, below, *fields, weights = call(
        functools.partial(pack_kernel, own, levels, n_lat),
        tuple(pltpu.with_memory_space_constraint(v, pltpu.HBM) for v in (x, b, c, h, coupling)),
        [real(len(FIRST), levels, LANES)] * 2 + [tile] * 4 + [whole] * len(FIELDS) + [rows],
        [(levels * own, LANES)] * 4 + [(1, levels - 1), padded, pltpu.SemaphoreType.DMA((5,))],
        [pl.BlockSpec(memory_space=pltpu.HBM)] * 5,
    )
    lat_a, lat_b = swap(lat_a, "lat_even"), swap(lat_b, "lat_odd")
    from_a, from_b = swap(to_a, "lon_even"), swap(to_b, "lon_odd")
    corners_a, corners_b = call(
        functools.partial(corner_kernel, own, levels, n_lat), (lat_a, lat_b), [tile] * 2
    )
    corners_a, corners_b = swap(corners_a, "lon_even"), swap(corners_b, "lon_odd")
    weights = everywhere(weights)
    k0, k1, k1_strip, to_a, to_b, *coefficients, shift = call(
        functools.partial(first_kernel, own, levels, columns, n_lat),
        (*fields, above, below, from_a, from_b, lat_a, lat_b, corners_a, corners_b, weights),
        [whole] * 3 + [real(FAR + 1, levels, LANES)] * 2 + [real(*extended)] * 4 + [real(1, LANES)],
        [extended] * 6,
    )
    from_a, from_b = swap(to_a, "lon_even"), swap(to_b, "lon_odd")
    k2, k3, k4, sums = call(
        functools.partial(second_kernel, own, levels, columns, n_lat),
        (k0, k1, k1_strip, from_a, from_b, *coefficients, above, below, shift),
        [whole] * 3 + [rows],
        [extended] * 4,
    )
    sums = everywhere(sums)
    out, rest = call(final_kernel, (sums, shift, x, c, k0, k1, k2, k3, k4), [whole] * 2)
    return out.reshape(right_side.shape), rest.reshape(right_side.shape)


def solution(mesh):
    spec = P(None, "lon", "lat")
    return jax.shard_map(
        program, mesh=mesh, in_specs=(spec, spec, spec, spec, P()), out_specs=(spec, spec), check_vma=False
    )
```

```python
import functools

import jax
import jax.numpy as jnp
from jax import lax
from jax.experimental import pallas as pl
from jax.experimental.pallas import tpu as pltpu
from jax.sharding import PartitionSpec as P


AXES = ("lon", "lat")
ITERS = 2
LANES = 128
NEAR, FAR = 2, 3
GROUP = 8
VMEM = pl.BlockSpec(memory_space=pltpu.VMEM)
FIRST = (("q", 1), ("q", 2), ("g", 1), ("d", 1), ("s", 1))
LATER = ("g", "d")
FIELDS = ("q", "g", "d", "s")


def swap_pairs(n_lon, n_lat):
    half = n_lon // 2

    def flat(move):
        pairs = []
        for i in range(n_lon):
            for j in range(n_lat):
                k, m = move(i, j)
                pairs.append((i * n_lat + j, k * n_lat + m))
        return pairs

    def lat_odd(i, j):
        if j == 0 or j == n_lat - 1:
            return (i + half) % n_lon, j
        return i, ((j + 1) ^ 1) - 1

    return {
        "lon_even": flat(lambda i, j: (i ^ 1, j)),
        "lon_odd": flat(lambda i, j: ((((i + 1) ^ 1) - 1) % n_lon, j)),
        "lat_even": flat(lambda i, j: (i, j ^ 1)),
        "lat_odd": flat(lat_odd),
    }


def plus(a, b):
    if a is None or b is None:
        return b if a is None else a
    return a + b


def times(a, b):
    return None if a is None or b is None else a * b


def add_scaled(a, scale, b):
    size = max(len(a), len(b))
    a, b = (list(v) + [None] * (size - len(v)) for v in (a, b))
    return [plus(x, times(scale, y)) for x, y in zip(a, b)]


def krylov_coefficients(first, mixed, rest, shift, one):
    def inner(a, b):
        total = times(times(a[0], b[0]), first)
        for x, others in ((a[0], b), (b[0], a)):
            for j in range(1, len(others)):
                total = plus(total, times(times(x, others[j]), mixed[j - 1]))
        for k in range(len(a) + len(b) - 3):
            part = None
            for i in range(1, len(a)):
                if 1 <= k + 2 - i < len(b):
                    part = plus(part, times(a[i], b[k + 2 - i]))
            total = plus(total, times(part, rest[k]))
        return total

    def image_of(a):
        return [None] + [plus(v, times(shift, a[k + 1]) if k + 1 < len(a) else None) for k, v in enumerate(a)]

    shadow = [one]
    residual = [one]
    direction = [one]
    solution = []
    rho = first
    for iteration in range(ITERS):
        image = image_of(direction)
        alpha = rho / inner(shadow, image)
        half = add_scaled(residual, -alpha, image)
        second = image_of(half)
        omega = inner(second, half) / inner(second, second)
        solution = add_scaled(solution, alpha, direction)
        solution = add_scaled(solution, omega, half)
        residual = add_scaled(half, -omega, second)
        if iteration + 1 < ITERS:
            rho_next = inner(shadow, half) - omega * inner(shadow, second)
            beta = rho_next / rho * (alpha / omega)
            direction = add_scaled(residual, beta, add_scaled(direction, -omega, image))
            rho = rho_next
    return solution, residual


PAIRS = (
    [(0, j) for j in range(2 * ITERS + 1)]
    + [(1 + k // 2, 1 + k - k // 2) for k in range(4 * ITERS - 1)]
)


def lanes_of(levels):
    return lax.broadcasted_iota(jnp.int32, (levels, LANES), 1)


def turn(value, shift):
    shift %= LANES
    return value if shift == 0 else pltpu.roll(value, shift, 1)


def plane(ref, column, columns, levels, shift=0):
    return ref.at[pl.ds((1 + shift) * columns + column, levels, stride=columns), :]


def clear_ends(ref, columns, levels):
    ref[0:columns, :] = jnp.zeros((columns, LANES), jnp.float32)
    ref[(levels + 1) * columns : (levels + 2) * columns, :] = jnp.zeros((columns, LANES), jnp.float32)


def column(ref, i, own, levels):
    return ref[pl.ds(i, levels, stride=own), :]


def shifted_rows(main, strip, lane):
    main_s, main_n = turn(main, -1), turn(main, 1)
    strip_s, strip_n = turn(strip, -1), turn(strip, 1)
    first, last = lane == 0, lane == LANES - 1
    return (
        jnp.where(last, strip_s, main_s) + jnp.where(first, strip_n, main_n),
        jnp.where(last, main_s, strip_s) + jnp.where(first, main_n, strip_n),
    )


def transformed(x, b, c, h, above, below):
    return {"q": c * x, "g": c * c, "d": (4.0 + h) + (above + below), "s": c * b}


def parity(size):
    i, j = lax.axis_index("lon"), lax.axis_index("lat")
    pole = (j == 0) | (j == size - 1)
    return 1 - lax.rem(i, 2), 1 - lax.rem(j, 2), pole


def pack_kernel(own, levels, n_lat, x_hbm, b_hbm, c_hbm, h_hbm, coupling_hbm, to_a, to_b, lat_a, lat_b, above,
                below, fq, fg, fd, fs, x, b, c, h, coupling, sem):
    copies = []
    moves = ((coupling_hbm, coupling), (x_hbm, x), (c_hbm, c), (h_hbm, h), (b_hbm, b))
    for k, (source, target) in enumerate(moves):
        copies.append(pltpu.make_async_copy(source, target, sem.at[k]))
        copies[-1].start()
    lane = lanes_of(levels)
    group = lane // GROUP
    groups = LANES // GROUP
    lon_even, lat_even, pole = parity(n_lat)
    store = dict(zip(FIELDS, (fq, fg, fd, fs)))
    copies[0].wait()
    wide = (levels, levels - 1)
    row, interface = (lax.broadcasted_iota(jnp.int32, wide, k) for k in (0, 1))
    strength = jnp.broadcast_to(coupling[...], wide)
    for out, k in ((below, row), (above, row - 1)):
        value = jnp.sum(jnp.where(interface == k, strength, 0.0), axis=1, keepdims=True)
        out[...] = jnp.broadcast_to(value, (levels, LANES))
    north = jnp.zeros((levels, LANES), jnp.float32)
    south = north
    for copy in copies[1:]:
        copy.wait()
    for i in range(own):
        values = transformed(
            column(x, i, own, levels),
            column(b, i, own, levels),
            column(c, i, own, levels),
            column(h, i, own, levels),
            above[...],
            below[...],
        )
        for f, name in enumerate(FIELDS):
            store[name][pl.ds(i, levels, stride=own), :] = values[name]
            slot = f * own + i
            rolled = turn(values[name], GROUP * slot)
            north = jnp.where(group == slot, rolled, north)
            south = jnp.where(group == (slot - 1) % groups, rolled, south)
    even = jnp.full((levels, LANES), lat_even, jnp.int32) == 1
    over = jnp.full((levels, LANES), pole.astype(jnp.int32), jnp.int32) == 1
    lat_a[...] = jnp.where(even, south, north)
    other = jnp.where(even, north, south)
    mirror = other
    for bit in (1, 2, 4):
        mirror = jnp.where((lane & bit) != 0, turn(mirror, bit), turn(mirror, -bit))
    mirror = jnp.where(even, turn(mirror, -GROUP), turn(mirror, GROUP))
    lat_b[...] = jnp.where(over, mirror, other)
    for k, (name, distance) in enumerate(FIRST):
        east, west = own - distance, distance - 1
        a = jnp.where(lon_even == 1, east, west)
        to_a[k] = store[name][pl.ds(a, levels, stride=own), :]
        to_b[k] = store[name][pl.ds(east + west - a, levels, stride=own), :]


def corner_kernel(own, levels, n_lat, lat_a, lat_b, to_a, to_b):
    lane = lanes_of(levels)
    quarter = (lane // GROUP) % own
    lon_even, lat_even, _ = parity(n_lat)
    even = jnp.full((levels, LANES), lat_even, jnp.int32) == 1
    lon = jnp.full((levels, LANES), lon_even, jnp.int32) == 1
    a, b = lat_a[...], lat_b[...]
    north, south = jnp.where(even, b, a), jnp.where(even, a, b)
    east = jnp.where(quarter >= own - NEAR, south, turn(north, GROUP * (1 - NEAR)))
    west = jnp.where(quarter < NEAR, south, turn(north, GROUP * (1 + NEAR)))
    to_a[...] = jnp.where(lon, east, west)
    to_b[...] = jnp.where(lon, west, east)


def lane_value(row, k):
    lane = lax.broadcasted_iota(jnp.int32, (1, LANES), 1)
    return jnp.sum(jnp.where(lane == k, row, 0.0), axis=1, keepdims=True)


def put_row(out, arrays):
    lane = lax.broadcasted_iota(jnp.int32, (1, LANES), 1)
    row = jnp.zeros((1, LANES), jnp.float32)
    for k, value in enumerate(arrays):
        row = jnp.where(lane == k, jnp.sum(value, keepdims=True), row)
    out[...] = jnp.broadcast_to(row[None], out.shape)


def total_row(gathered):
    return jnp.sum(gathered[...], axis=0)


class Extended:
    def __init__(self, columns, levels, d, g, above, below, lane, far=None):
        self.columns, self.levels = columns, levels
        self.far = far
        self.d, self.g = d, g
        self.above, self.below, self.lane = above, below, lane

    def at(self, pair, k, e, shift=0):
        return plane(pair[k], e, self.columns, self.levels, shift)[...]

    def coefficient(self, name, k, e):
        edges = (FAR - NEAR, self.columns - 1 - FAR + NEAR)
        if self.far is not None and k == 0 and e in edges:
            return self.far[LATER.index(name), edges.index(e)]
        return self.at(self.g if name == "g" else self.d, k, e)

    def put(self, pair, k, e, value):
        plane(pair[k], e, self.columns, self.levels)[...] = value

    def stencil(self, pair, e, strips=True):
        main, strip = self.at(pair, 0, e), self.at(pair, 1, e)
        near = shifted_rows(main, strip, self.lane)
        out = []
        for k, q in enumerate((main, strip) if strips else (main,)):
            side = self.at(pair, k, e - 1) + self.at(pair, k, e + 1)
            levels = self.below[...] * self.at(pair, k, e, 1) + self.above[...] * self.at(pair, k, e, -1)
            out.append((q, self.coefficient("d", k, e) * q - (side + near[k]) - levels))
        return out


def first_kernel(own, levels, columns, n_lat, fq, fg, fd, fs, above, below, from_a, from_b, lat_a, lat_b,
                 corners_a, corners_b, k0, k1, k1_strip, to_a, to_b, g_main, g_strip, d_main, d_strip,
                 out, qa_main, qa_strip, qb_main, qb_strip, s_main, s_strip):
    lane = lanes_of(levels)
    low = lane < LANES // 2
    lon_even, lat_even, _ = parity(n_lat)
    even = jnp.full((levels, LANES), lat_even, jnp.int32) == 1
    qa, qb = (qa_main, qa_strip), (qb_main, qb_strip)
    where_to = {"q": qa, "g": (g_main, g_strip), "d": (d_main, d_strip), "s": (s_main, s_strip)}
    ext = Extended(columns, levels, where_to["d"], where_to["g"], above, below, lane)
    for ref in (*qa, *qb):
        clear_ends(ref, columns, levels)

    def unpack(north, south, name, i):
        back = -GROUP * (FIELDS.index(name) * own + i)
        return jnp.where(low, turn(south, back), turn(north, back))

    fields = dict(zip(FIELDS, (fq, fg, fd, fs)))
    a, b = lat_a[...], lat_b[...]
    north, south = jnp.where(even, b, a), jnp.where(even, a, b)
    for name in FIELDS:
        for i in range(own):
            ext.put(where_to[name], 0, FAR + i, column(fields[name], i, own, levels))
            ext.put(where_to[name], 1, FAR + i, unpack(north, south, name, i))
    for block, corner, east in ((from_a, corners_a, lon_even), (from_b, corners_b, 1 - lon_even)):
        is_east = jnp.full((levels, LANES), east, jnp.int32) == 1
        tile = corner[...]
        north = jnp.where(is_east, turn(tile, -GROUP * (1 + NEAR)), turn(tile, -GROUP * (1 - NEAR)))
        for k, (name, distance) in enumerate(FIRST + tuple((name, NEAR) for name in LATER)):
            e = jnp.where(east == 1, FAR + own - 1 + distance, FAR - distance)
            if k < len(FIRST):
                ext.put(where_to[name], 0, e, block[k])
            strip = jnp.where(
                is_east, unpack(north, tile, name, distance - 1), unpack(north, tile, name, own - distance)
            )
            ext.put(where_to[name], 1, e, strip)
    for e in range(FAR - 1, FAR + own + 1):
        for k, (_, image) in enumerate(ext.stencil(qa, e)):
            value = ext.at(where_to["s"], k, e) - ext.at(where_to["g"], k, e) * image
            ext.put(qb, k, e, value)
            if k == 0 and FAR <= e < FAR + own:
                k0[pl.ds(e - FAR, levels, stride=own), :] = value
    mixed = jnp.zeros((levels, LANES), jnp.float32)
    square = mixed
    for e in range(FAR, FAR + own):
        for k, (q, image) in enumerate(ext.stencil(qb, e)):
            scale = ext.at(where_to["g"], k, e)
            value = scale * image
            target = k1 if k == 0 else k1_strip
            target[pl.ds(e - FAR, levels, stride=own), :] = value
            if k == 0:
                mixed = mixed + q * image
                square = square + value * image
    put_row(out, (mixed, square))
    for message, side in ((to_a, lon_even), (to_b, 1 - lon_even)):
        packed = jnp.zeros((levels, LANES), jnp.float32)
        for distance in range(1, FAR + 1):
            i = jnp.where(side == 1, own - distance, distance - 1)
            message[distance - 1] = k1[pl.ds(i, levels, stride=own), :]
            offset = 2 * GROUP * (distance - 1) + GROUP
            rolled = turn(k1_strip[pl.ds(i, levels, stride=own), :], offset)
            packed = jnp.where(lane // (2 * GROUP) == distance - 1, rolled, packed)
        message[FAR] = packed
        i = jnp.where(side == 1, own - NEAR, NEAR - 1)
        for k, name in enumerate(LATER):
            message[FAR + 1 + k] = column(fields[name], i, own, levels)


def second_kernel(own, levels, columns, n_lat, k0, k1, k1_strip, from_a, from_b, g_main, g_strip, d_main, d_strip,
                  above, below, shift_sums, k2, k3, k4, out, shift_row, qa_main, qa_strip, qb_main, qb_strip, far):
    lane = lanes_of(levels)
    lon_even, _, _ = parity(n_lat)
    qa, qb = (qa_main, qa_strip), (qb_main, qb_strip)
    g = (g_main, g_strip)
    ext = Extended(columns, levels, (d_main, d_strip), g, above, below, lane, far)
    for ref in (*qa, *qb):
        clear_ends(ref, columns, levels)
    row = total_row(shift_sums)
    mixed, square = lane_value(row, 0), lane_value(row, 1)
    shift = jnp.where(mixed > 0.0, square / jnp.where(mixed > 0.0, mixed, 1.0), 1.0)
    shift_row[...] = jnp.broadcast_to(shift, shift_row.shape)
    shift = jnp.broadcast_to(shift, (levels, LANES))
    for i in range(own):
        ext.put(qa, 0, FAR + i, column(k1, i, own, levels))
        ext.put(qa, 1, FAR + i, column(k1_strip, i, own, levels))
    for block, east in ((from_a, lon_even), (from_b, 1 - lon_even)):
        for distance in range(1, FAR + 1):
            e = jnp.where(east == 1, FAR + own - 1 + distance, FAR - distance)
            ext.put(qa, 0, e, block[distance - 1])
            ext.put(qa, 1, e, turn(block[FAR], -(2 * GROUP * (distance - 1) + GROUP)))
        for k in range(len(LATER)):
            far[k, east] = block[FAR + 1 + k]
    source, target = qa, qb
    for step, reach in ((0, FAR - 1), (1, FAR - 2)):
        for e in range(FAR - reach, FAR + own + reach):
            for k, (q, image) in enumerate(ext.stencil(source, e)):
                value = ext.coefficient("g", k, e) * image - shift * q
                ext.put(target, k, e, value)
                if k == 0 and FAR <= e < FAR + own:
                    (k2, k3)[step][pl.ds(e - FAR, levels, stride=own), :] = value
        source, target = target, source
    sums = [jnp.zeros((levels, LANES), jnp.float32) for _ in PAIRS]
    for i in range(own):
        e = FAR + i
        ((q, image),) = ext.stencil(source, e, strips=False)
        scale = ext.at(g, 0, e)
        last = scale * image - shift * q
        k4[pl.ds(i, levels, stride=own), :] = last
        v = [column(k0, i, own, levels), column(k1, i, own, levels), column(k2, i, own, levels), q, last]
        w = 1.0 / scale
        lead = [a * w for a in v]
        for k, (a, b) in enumerate(PAIRS):
            sums[k] = sums[k] + lead[a] * v[b]
    put_row(out, sums)


def final_kernel(sums, shift_row, x, c, k0, k1, k2, k3, k4, out, rest):
    row = total_row(sums)
    first, *others = [lane_value(row, k) for k in range(len(PAIRS))]
    shift = lane_value(shift_row[...], 0)
    one = jnp.ones((1, 1), jnp.float32)
    solution, residual = krylov_coefficients(first, others[: 2 * ITERS], others[2 * ITERS :], shift, one)
    vectors = (k0, k1, k2, k3, k4)
    inverse = 1.0 / c[...]

    def combined(coefficients):
        total = None
        for a, v in zip(coefficients, vectors):
            term = a * v[...]
            total = term if total is None else total + term
        return total * inverse

    out[...] = x[...] + combined(solution)
    rest[...] = combined(residual)


def program(right_side, first_guess, cell_scale, helmholtz_term, vertical_coupling):
    n_lon, n_lat = lax.axis_size("lon"), lax.axis_size("lat")
    levels, own, width = right_side.shape
    assert width == LANES and own == 2 * NEAR >= FAR and len(FIELDS) * own * GROUP == LANES
    assert n_lon % 4 == 0 and n_lat % 2 == 0
    columns = own + 2 * FAR
    pairs = swap_pairs(n_lon, n_lat)
    coupling = vertical_coupling.reshape(1, levels - 1)
    b, x, c, h = (v.reshape(levels * own, LANES) for v in (right_side, first_guess, cell_scale, helmholtz_term))

    def real(*shape):
        return jax.ShapeDtypeStruct(shape, jnp.float32)

    def call(kernel, ins, outs, scratch=(), specs=None, grant=32 * 1024 * 1024):
        return pl.pallas_call(
            kernel,
            out_shape=tuple(outs) if len(outs) > 1 else outs[0],
            in_specs=specs or [VMEM] * len(ins),
            out_specs=tuple([VMEM] * len(outs)) if len(outs) > 1 else VMEM,
            scratch_shapes=[pltpu.VMEM(s, jnp.float32) if isinstance(s, tuple) else s for s in scratch],
            compiler_params=pltpu.CompilerParams(vmem_limit_bytes=grant),
        )(*ins)

    def swap(value, name):
        return lax.ppermute(value, AXES, pairs[name])

    def everywhere(rows):
        return lax.all_to_all(rows, AXES, 0, 0, tiled=True)

    whole = real(levels * own, LANES)
    tile = real(levels, LANES)
    rows = real(n_lon * n_lat, 1, LANES)
    extended = ((levels + 2) * columns, LANES)

    to_a, to_b, lat_a, lat_b, above, below, *fields = call(
        functools.partial(pack_kernel, own, levels, n_lat),
        tuple(pltpu.with_memory_space_constraint(v, pltpu.HBM) for v in (x, b, c, h, coupling)),
        [real(len(FIRST), levels, LANES)] * 2 + [tile] * 4 + [whole] * len(FIELDS),
        [(levels * own, LANES)] * 4 + [(1, levels - 1), pltpu.SemaphoreType.DMA((5,))],
        [pl.BlockSpec(memory_space=pltpu.HBM)] * 5,
    )
    lat_a, lat_b = swap(lat_a, "lat_even"), swap(lat_b, "lat_odd")
    from_a = swap(to_a, "lon_even")
    from_b = swap(to_b, "lon_odd")
    corners_a, corners_b = call(
        functools.partial(corner_kernel, own, levels, n_lat), (lat_a, lat_b), [tile] * 2
    )
    corners_a, corners_b = swap(corners_a, "lon_even"), swap(corners_b, "lon_odd")
    k0, k1, k1_strip, to_a, to_b, *coefficients, shift_sums = call(
        functools.partial(first_kernel, own, levels, columns, n_lat),
        (*fields, above, below, from_a, from_b, lat_a, lat_b, corners_a, corners_b),
        [whole] * 3 + [real(FAR + 1 + len(LATER), levels, LANES)] * 2 + [real(*extended)] * 4 + [rows],
        [extended] * 6,
    )
    from_a = swap(to_a, "lon_even")
    from_b = swap(to_b, "lon_odd")
    shift_sums = everywhere(shift_sums)
    k2, k3, k4, sums, shift = call(
        functools.partial(second_kernel, own, levels, columns, n_lat),
        (k0, k1, k1_strip, from_a, from_b, *coefficients, above, below, shift_sums),
        [whole] * 3 + [rows, real(1, LANES)],
        [extended] * 4 + [(len(LATER), 2, levels, LANES)],
    )
    sums = everywhere(sums)
    out, rest = call(final_kernel, (sums, shift, x, c, k0, k1, k2, k3, k4), [whole] * 2)
    return out.reshape(right_side.shape), rest.reshape(right_side.shape)


def solution(mesh):
    spec = P(None, "lon", "lat")
    return jax.shard_map(
        program, mesh=mesh, in_specs=(spec, spec, spec, spec, P()), out_specs=(spec, spec), check_vma=False
    )
```

```python
import functools

import jax
import jax.numpy as jnp
from jax import lax
from jax.experimental import pallas as pl
from jax.experimental.pallas import tpu as pltpu
from jax.sharding import PartitionSpec as P


AXES = ("lon", "lat")
ITERS = 2
LANES = 128
SUBLANES = 8
NEAR, FAR = 2, 3
GROUP = 8
VMEM = pl.BlockSpec(memory_space=pltpu.VMEM)
FIRST = (("q", 1), ("q", 2), ("g", 1), ("d", 1), ("s", 1))
LATER = ("g", "d")
FIELDS = ("q", "g", "d", "s")


def swap_pairs(n_lon, n_lat):
    half = n_lon // 2

    def flat(move):
        pairs = []
        for i in range(n_lon):
            for j in range(n_lat):
                k, m = move(i, j)
                pairs.append((i * n_lat + j, k * n_lat + m))
        return pairs

    def lat_odd(i, j):
        if j == 0 or j == n_lat - 1:
            return (i + half) % n_lon, j
        return i, ((j + 1) ^ 1) - 1

    return {
        "lon_even": flat(lambda i, j: (i ^ 1, j)),
        "lon_odd": flat(lambda i, j: ((((i + 1) ^ 1) - 1) % n_lon, j)),
        "lat_even": flat(lambda i, j: (i, j ^ 1)),
        "lat_odd": flat(lat_odd),
    }


def plus(a, b):
    if a is None or b is None:
        return b if a is None else a
    return a + b


def times(a, b):
    return None if a is None or b is None else a * b


def add_scaled(a, scale, b):
    size = max(len(a), len(b))
    a, b = (list(v) + [None] * (size - len(v)) for v in (a, b))
    return [plus(x, times(scale, y)) for x, y in zip(a, b)]


def krylov_coefficients(first, mixed, rest, shift, one):
    def inner(a, b):
        total = times(times(a[0], b[0]), first)
        for x, others in ((a[0], b), (b[0], a)):
            for j in range(1, len(others)):
                total = plus(total, times(times(x, others[j]), mixed[j - 1]))
        for k in range(len(a) + len(b) - 3):
            part = None
            for i in range(1, len(a)):
                if 1 <= k + 2 - i < len(b):
                    part = plus(part, times(a[i], b[k + 2 - i]))
            total = plus(total, times(part, rest[k]))
        return total

    def image_of(a):
        return [None] + [plus(v, times(shift, a[k + 1]) if k + 1 < len(a) else None) for k, v in enumerate(a)]

    shadow = [one]
    residual = [one]
    direction = [one]
    solution = []
    rho = first
    for iteration in range(ITERS):
        image = image_of(direction)
        alpha = rho / inner(shadow, image)
        half = add_scaled(residual, -alpha, image)
        second = image_of(half)
        omega = inner(second, half) / inner(second, second)
        solution = add_scaled(solution, alpha, direction)
        solution = add_scaled(solution, omega, half)
        residual = add_scaled(half, -omega, second)
        if iteration + 1 < ITERS:
            rho_next = inner(shadow, half) - omega * inner(shadow, second)
            beta = rho_next / rho * (alpha / omega)
            direction = add_scaled(residual, beta, add_scaled(direction, -omega, image))
            rho = rho_next
    return solution, residual


PAIRS = (
    [(0, j) for j in range(2 * ITERS + 1)]
    + [(1 + k // 2, 1 + k - k // 2) for k in range(4 * ITERS - 1)]
)


def lanes_of(levels):
    return lax.broadcasted_iota(jnp.int32, (levels, LANES), 1)


def turn(value, shift):
    shift %= LANES
    return value if shift == 0 else pltpu.roll(value, shift, 1)


def plane(ref, column, columns, levels, shift=0):
    return ref.at[pl.ds((1 + shift) * columns + column, levels, stride=columns), :]


def clear_ends(ref, columns, levels):
    ref[0:columns, :] = jnp.zeros((columns, LANES), jnp.float32)
    ref[(levels + 1) * columns : (levels + 2) * columns, :] = jnp.zeros((columns, LANES), jnp.float32)


def column(ref, i, own, levels):
    return ref[pl.ds(i, levels, stride=own), :]


def shifted_rows(main, strip, lane, strips=True):
    main_s, main_n = turn(main, -1), turn(main, 1)
    strip_s, strip_n = turn(strip, -1), turn(strip, 1)
    first, last = lane == 0, lane == LANES - 1
    out = [jnp.where(last, strip_s, main_s) + jnp.where(first, strip_n, main_n)]
    if strips:
        out.append(jnp.where(last, main_s, strip_s) + jnp.where(first, main_n, strip_n))
    return out


def transformed(x, b, c, h, above, below):
    return {"q": c * x, "g": c * c, "d": (4.0 + h) + (above + below), "s": c * b}


def parity(size):
    i, j = lax.axis_index("lon"), lax.axis_index("lat")
    pole = (j == 0) | (j == size - 1)
    return 1 - lax.rem(i, 2), 1 - lax.rem(j, 2), pole


def pack_kernel(own, levels, n_lat, x_hbm, b_hbm, c_hbm, h_hbm, coupling_hbm, to_a, to_b, lat_a, lat_b, above,
                below, fq, fg, fd, fs, x, b, c, h, coupling, sem):
    copies = []
    moves = ((coupling_hbm, coupling), (x_hbm, x), (c_hbm, c), (h_hbm, h), (b_hbm, b))
    for k, (source, target) in enumerate(moves):
        copies.append(pltpu.make_async_copy(source, target, sem.at[k]))
        copies[-1].start()
    lane = lanes_of(levels)
    group = lane // GROUP
    groups = LANES // GROUP
    lon_even, lat_even, pole = parity(n_lat)
    store = dict(zip(FIELDS, (fq, fg, fd, fs)))
    copies[0].wait()
    wide = (levels, levels - 1)
    row, interface = (lax.broadcasted_iota(jnp.int32, wide, k) for k in (0, 1))
    strength = jnp.broadcast_to(coupling[...], wide)
    for out, k in ((below, row), (above, row - 1)):
        value = jnp.sum(jnp.where(interface == k, strength, 0.0), axis=1, keepdims=True)
        out[...] = jnp.broadcast_to(value, (levels, LANES))
    north = jnp.zeros((levels, LANES), jnp.float32)
    south = north
    for copy in copies[1:]:
        copy.wait()
    for i in range(own):
        values = transformed(
            column(x, i, own, levels),
            column(b, i, own, levels),
            column(c, i, own, levels),
            column(h, i, own, levels),
            above[...],
            below[...],
        )
        for f, name in enumerate(FIELDS):
            store[name][pl.ds(i, levels, stride=own), :] = values[name]
            slot = f * own + i
            rolled = turn(values[name], GROUP * slot)
            north = jnp.where(group == slot, rolled, north)
            south = jnp.where(group == (slot - 1) % groups, rolled, south)
    even = jnp.full((levels, LANES), lat_even, jnp.int32) == 1
    over = jnp.full((levels, LANES), pole.astype(jnp.int32), jnp.int32) == 1
    lat_a[...] = jnp.where(even, south, north)
    other = jnp.where(even, north, south)
    mirror = other
    for bit in (1, 2, 4):
        mirror = jnp.where((lane & bit) != 0, turn(mirror, bit), turn(mirror, -bit))
    mirror = jnp.where(even, turn(mirror, -GROUP), turn(mirror, GROUP))
    lat_b[...] = jnp.where(over, mirror, other)
    for k, (name, distance) in enumerate(FIRST):
        east, west = own - distance, distance - 1
        a = jnp.where(lon_even == 1, east, west)
        to_a[k] = store[name][pl.ds(a, levels, stride=own), :]
        to_b[k] = store[name][pl.ds(east + west - a, levels, stride=own), :]


def corner_kernel(own, levels, n_lat, lat_a, lat_b, to_a, to_b):
    lane = lanes_of(levels)
    quarter = (lane // GROUP) % own
    lon_even, lat_even, _ = parity(n_lat)
    even = jnp.full((levels, LANES), lat_even, jnp.int32) == 1
    lon = jnp.full((levels, LANES), lon_even, jnp.int32) == 1
    a, b = lat_a[...], lat_b[...]
    north, south = jnp.where(even, b, a), jnp.where(even, a, b)
    east = jnp.where(quarter >= own - NEAR, south, turn(north, GROUP * (1 - NEAR)))
    west = jnp.where(quarter < NEAR, south, turn(north, GROUP * (1 + NEAR)))
    to_a[...] = jnp.where(lon, east, west)
    to_b[...] = jnp.where(lon, west, east)


def lane_value(row, k):
    lane = lax.broadcasted_iota(jnp.int32, (1, LANES), 1)
    return jnp.sum(jnp.where(lane == k, row, 0.0), axis=1, keepdims=True)


def put_row(out, arrays):
    lane = lax.broadcasted_iota(jnp.int32, (1, LANES), 1)
    row = jnp.zeros((1, LANES), jnp.float32)
    for k, value in enumerate(arrays):
        row = jnp.where(lane == k, value.total(), row)
    out[...] = jnp.broadcast_to(row[None], out.shape)


def total_row(gathered):
    return jnp.sum(gathered[...], axis=0)


class Extended:
    def __init__(self, columns, levels, d, g, above, below, far=None):
        self.columns, self.levels = columns, levels
        self.d, self.g = d, g
        self.above, self.below = above, below
        self.far = far

    def at(self, pair, k, e, rows, shift=0):
        start, count = rows
        return pair[k][pl.ds((1 + start + shift) * self.columns + e, count, stride=self.columns), :]

    def set(self, pair, k, e, rows, value):
        start, count = rows
        pair[k][pl.ds((1 + start) * self.columns + e, count, stride=self.columns), :] = value

    def put(self, pair, k, e, value):
        self.set(pair, k, e, (0, self.levels), value)

    def coefficient(self, name, k, e, rows):
        edges = (FAR - NEAR, self.columns - 1 - FAR + NEAR)
        if self.far is not None and k == 0 and e in edges:
            start, count = rows
            return self.far[LATER.index(name), edges.index(e), start : start + count, :]
        return self.at(self.g if name == "g" else self.d, k, e, rows)

    def sweep(self, pair, first, last, strips=True):
        for start in range(0, self.levels, SUBLANES):
            rows = start, min(SUBLANES, self.levels - start)
            lane = lanes_of(rows[1])
            above, below = (ref[start : start + rows[1], :] for ref in (self.above, self.below))
            center = {}

            def middle(k, e):
                if (k, e) not in center:
                    center[k, e] = self.at(pair, k, e, rows)
                return center[k, e]

            for e in range(first, last + 1):
                near = shifted_rows(middle(0, e), middle(1, e), lane, strips)
                out = []
                for k in range(1 + strips):
                    q = middle(k, e)
                    side = middle(k, e - 1) + middle(k, e + 1)
                    levels = below * self.at(pair, k, e, rows, 1) + above * self.at(pair, k, e, rows, -1)
                    out.append((q, self.coefficient("d", k, e, rows) * q - (side + near[k]) - levels))
                yield rows, e, out


class Sums:
    def __init__(self):
        self.parts = {}

    def add(self, value):
        count = value.shape[0]
        self.parts[count] = self.parts[count] + value if count in self.parts else value

    def total(self):
        return sum(jnp.sum(v, keepdims=True) for v in self.parts.values())


def own_rows(i, own, rows):
    start, count = rows
    return pl.ds(start * own + i, count, stride=own), slice(None)


def own_kernel(own, levels, columns, n_lat, fq, fg, fd, fs, lat_a, lat_b, *outs):
    group = lanes_of(levels) // GROUP
    _, lat_even, _ = parity(n_lat)
    even = jnp.full((levels, LANES), lat_even, jnp.int32) == 1
    a, b = lat_a[...], lat_b[...]
    north, south = jnp.where(even, b, a), jnp.where(even, a, b)
    for f, field in enumerate((fq, fg, fd, fs)):
        main, strip = outs[2 * f : 2 * f + 2]
        if f == 0:
            clear_ends(main, columns, levels)
            clear_ends(strip, columns, levels)
        for i in range(own):
            slot = f * own + i
            plane(main, FAR + i, columns, levels)[...] = column(field, i, own, levels)
            edges = turn(jnp.where(group == slot, south, north), -GROUP * slot)
            plane(strip, FAR + i, columns, levels)[...] = edges


def first_kernel(own, levels, columns, n_lat, fg, fd, above, below, from_a, from_b, corners_a, corners_b, *refs):
    extended = refs[8:16]
    k0, k1, k1_strip, to_a, to_b, out, qb_main, qb_strip = refs[16:]
    lane = lanes_of(levels)
    low = lane < LANES // 2
    lon_even, _, _ = parity(n_lat)
    pairs = {name: extended[2 * f : 2 * f + 2] for f, name in enumerate(FIELDS)}
    qa, qb = pairs["q"], (qb_main, qb_strip)
    ext = Extended(columns, levels, pairs["d"], pairs["g"], above, below)
    for ref in qb:
        clear_ends(ref, columns, levels)
    for block, corner, east in ((from_a, corners_a, lon_even), (from_b, corners_b, 1 - lon_even)):
        tile = corner[...]
        for k, (name, distance) in enumerate(FIRST + tuple((name, NEAR) for name in LATER)):
            e = jnp.where(east == 1, FAR + own - 1 + distance, FAR - distance)
            if k < len(FIRST):
                ext.put(pairs[name], 0, e, block[k])
            slot = FIELDS.index(name) * own + jnp.where(east == 1, distance - 1, own - distance)
            south = lax.rem(2 * LANES - GROUP * slot, LANES)
            north = lax.rem(south + LANES - GROUP * jnp.where(east == 1, 1 + NEAR, 1 - NEAR), LANES)
            ext.put(pairs[name], 1, e, jnp.where(low, pltpu.roll(tile, south, 1), pltpu.roll(tile, north, 1)))
    for rows, e, tiles in ext.sweep(qa, FAR - 1, FAR + own):
        for k, (_, image) in enumerate(tiles):
            value = ext.at(pairs["s"], k, e, rows) - ext.at(pairs["g"], k, e, rows) * image
            ext.set(qb, k, e, rows, value)
            if k == 0 and FAR <= e < FAR + own:
                k0[own_rows(e - FAR, own, rows)] = value
    mixed, square = Sums(), Sums()
    for rows, e, tiles in ext.sweep(qb, FAR, FAR + own - 1):
        for k, (q, image) in enumerate(tiles):
            value = ext.at(pairs["g"], k, e, rows) * image
            (k1, k1_strip)[k][own_rows(e - FAR, own, rows)] = value
            if k == 0:
                mixed.add(q * image)
                square.add(value * image)
    put_row(out, (mixed, square))
    for message, side in ((to_a, lon_even), (to_b, 1 - lon_even)):
        packed = jnp.zeros((levels, LANES), jnp.float32)
        for distance in range(1, FAR + 1):
            i = jnp.where(side == 1, own - distance, distance - 1)
            message[distance - 1] = column(k1, i, own, levels)
            offset = 2 * GROUP * (distance - 1) + GROUP
            rolled = turn(column(k1_strip, i, own, levels), offset)
            packed = jnp.where(lane // (2 * GROUP) == distance - 1, rolled, packed)
        message[FAR] = packed
        i = jnp.where(side == 1, own - NEAR, NEAR - 1)
        for k, field in enumerate((fg, fd)):
            message[FAR + 1 + k] = column(field, i, own, levels)


def second_kernel(own, levels, columns, n_lat, k0, k1, k1_strip, from_a, from_b, g_main, g_strip, d_main, d_strip,
                  above, below, shift_sums, k2, k3, k4, out, shift_row, qa_main, qa_strip, qb_main, qb_strip, far):
    lon_even, _, _ = parity(n_lat)
    qa, qb = (qa_main, qa_strip), (qb_main, qb_strip)
    g = (g_main, g_strip)
    ext = Extended(columns, levels, (d_main, d_strip), g, above, below, far)
    for ref in (*qa, *qb):
        clear_ends(ref, columns, levels)
    row = total_row(shift_sums)
    mixed, square = lane_value(row, 0), lane_value(row, 1)
    shift = jnp.where(mixed > 0.0, square / jnp.where(mixed > 0.0, mixed, 1.0), 1.0)
    shift_row[...] = jnp.broadcast_to(shift, shift_row.shape)
    shift = jnp.broadcast_to(shift, (SUBLANES, LANES))
    for i in range(own):
        ext.put(qa, 0, FAR + i, column(k1, i, own, levels))
        ext.put(qa, 1, FAR + i, column(k1_strip, i, own, levels))
    for block, east in ((from_a, lon_even), (from_b, 1 - lon_even)):
        for distance in range(1, FAR + 1):
            e = jnp.where(east == 1, FAR + own - 1 + distance, FAR - distance)
            ext.put(qa, 0, e, block[distance - 1])
            ext.put(qa, 1, e, turn(block[FAR], -(2 * GROUP * (distance - 1) + GROUP)))
        for k in range(len(LATER)):
            far[k, east] = block[FAR + 1 + k]
    for rows, e, tiles in ext.sweep(qa, FAR - NEAR, FAR + own - 1 + NEAR):
        for k, (q, image) in enumerate(tiles):
            value = ext.coefficient("g", k, e, rows) * image - shift[: rows[1]] * q
            ext.set(qb, k, e, rows, value)
            if k == 0 and FAR <= e < FAR + own:
                k2[own_rows(e - FAR, own, rows)] = value
    for rows, e, tiles in ext.sweep(qb, FAR - 1, FAR + own):
        for k, (q, image) in enumerate(tiles):
            value = ext.at(g, k, e, rows) * image - shift[: rows[1]] * q
            ext.set(qa, k, e, rows, value)
            if k == 0 and FAR <= e < FAR + own:
                k3[own_rows(e - FAR, own, rows)] = value
    sums = [Sums() for _ in PAIRS]
    for rows, e, ((q, image),) in ext.sweep(qa, FAR, FAR + own - 1, strips=False):
        place = own_rows(e - FAR, own, rows)
        scale = ext.at(g, 0, e, rows)
        last = scale * image - shift[: rows[1]] * q
        k4[place] = last
        v = [k0[place], k1[place], k2[place], q, last]
        w = 1.0 / scale
        lead = [a * w for a in v]
        for total, (a, b) in zip(sums, PAIRS):
            total.add(lead[a] * v[b])
    put_row(out, sums)


def final_kernel(sums, shift_row, x, c, k0, k1, k2, k3, k4, out, rest):
    row = total_row(sums)
    first, *others = [lane_value(row, k) for k in range(len(PAIRS))]
    shift = lane_value(shift_row[...], 0)
    one = jnp.ones((1, 1), jnp.float32)
    solution, residual = krylov_coefficients(first, others[: 2 * ITERS], others[2 * ITERS :], shift, one)
    vectors = (k0, k1, k2, k3, k4)
    inverse = 1.0 / c[...]

    def combined(coefficients):
        total = None
        for a, v in zip(coefficients, vectors):
            term = a * v[...]
            total = term if total is None else total + term
        return total * inverse

    out[...] = x[...] + combined(solution)
    rest[...] = combined(residual)


def program(right_side, first_guess, cell_scale, helmholtz_term, vertical_coupling):
    n_lon, n_lat = lax.axis_size("lon"), lax.axis_size("lat")
    levels, own, width = right_side.shape
    assert width == LANES and own == 2 * NEAR >= FAR and len(FIELDS) * own * GROUP == LANES
    assert n_lon % 4 == 0 and n_lat % 2 == 0
    columns = own + 2 * FAR
    pairs = swap_pairs(n_lon, n_lat)
    coupling = vertical_coupling.reshape(1, levels - 1)
    b, x, c, h = (v.reshape(levels * own, LANES) for v in (right_side, first_guess, cell_scale, helmholtz_term))

    def real(*shape):
        return jax.ShapeDtypeStruct(shape, jnp.float32)

    def call(kernel, ins, outs, scratch=(), specs=None, aliases=()):
        return pl.pallas_call(
            kernel,
            out_shape=tuple(outs) if len(outs) > 1 else outs[0],
            in_specs=specs or [VMEM] * len(ins),
            out_specs=tuple([VMEM] * len(outs)) if len(outs) > 1 else VMEM,
            scratch_shapes=[pltpu.VMEM(s, jnp.float32) if isinstance(s, tuple) else s for s in scratch],
            compiler_params=pltpu.CompilerParams(vmem_limit_bytes=32 * 1024 * 1024),
            input_output_aliases=dict(aliases),
        )(*ins)

    def swap(value, name):
        return lax.ppermute(value, AXES, pairs[name])

    def everywhere(rows):
        return lax.all_to_all(rows, AXES, 0, 0, tiled=True)

    whole = real(levels * own, LANES)
    tile = real(levels, LANES)
    rows = real(n_lon * n_lat, 1, LANES)
    extended = ((levels + 2) * columns, LANES)

    to_a, to_b, lat_a, lat_b, above, below, *fields = call(
        functools.partial(pack_kernel, own, levels, n_lat),
        tuple(pltpu.with_memory_space_constraint(v, pltpu.HBM) for v in (x, b, c, h, coupling)),
        [real(len(FIRST), levels, LANES)] * 2 + [tile] * 4 + [whole] * len(FIELDS),
        [(levels * own, LANES)] * 4 + [(1, levels - 1), pltpu.SemaphoreType.DMA((5,))],
        [pl.BlockSpec(memory_space=pltpu.HBM)] * 5,
    )
    lat_a = swap(lat_a, "lat_even")
    lat_b = swap(lat_b, "lat_odd")
    from_a = swap(to_a, "lon_even")
    from_b = swap(to_b, "lon_odd")
    corners_a, corners_b = call(
        functools.partial(corner_kernel, own, levels, n_lat), (lat_a, lat_b), [tile] * 2
    )
    corners_a = swap(corners_a, "lon_even")
    corners_b = swap(corners_b, "lon_odd")
    buffers = call(
        functools.partial(own_kernel, own, levels, columns, n_lat),
        (*fields, lat_a, lat_b),
        [real(*extended)] * 2 * len(FIELDS),
    )
    ins = (fields[1], fields[2], above, below, from_a, from_b, corners_a, corners_b, *buffers)
    *buffers, k0, k1, k1_strip, to_a, to_b, shift_sums = call(
        functools.partial(first_kernel, own, levels, columns, n_lat),
        ins,
        [real(*extended)] * 2 * len(FIELDS)
        + [whole] * 3
        + [real(FAR + 1 + len(LATER), levels, LANES)] * 2
        + [rows],
        [extended] * 2,
        aliases=[(len(ins) - 2 * len(FIELDS) + k, k) for k in range(2 * len(FIELDS))],
    )
    coefficients = buffers[2:6]
    from_a = swap(to_a, "lon_even")
    from_b = swap(to_b, "lon_odd")
    shift_sums = everywhere(shift_sums)
    k2, k3, k4, sums, shift = call(
        functools.partial(second_kernel, own, levels, columns, n_lat),
        (k0, k1, k1_strip, from_a, from_b, *coefficients, above, below, shift_sums),
        [whole] * 3 + [rows, real(1, LANES)],
        [extended] * 4 + [(len(LATER), 2, levels, LANES)],
    )
    sums = everywhere(sums)
    out, rest = call(final_kernel, (sums, shift, x, c, k0, k1, k2, k3, k4), [whole] * 2)
    return out.reshape(right_side.shape), rest.reshape(right_side.shape)


def solution(mesh):
    spec = P(None, "lon", "lat")
    return jax.shard_map(
        program, mesh=mesh, in_specs=(spec, spec, spec, spec, P()), out_specs=(spec, spec), check_vma=False
    )
```

```python
import functools

import jax
import jax.numpy as jnp
from jax import lax
from jax.experimental import pallas as pl
from jax.experimental.pallas import tpu as pltpu
from jax.sharding import PartitionSpec as P


AXES = ("lon", "lat")
ITERS = 2
LANES = 128
SUBLANES = 8
NEAR, FAR = 2, 3
GROUP = 8
VMEM = pl.BlockSpec(memory_space=pltpu.VMEM)
FIRST = ("q", "s", "g")
STRIPS = (("q", 1), ("q", 2), ("g", 1), ("d", 1), ("s", 1))
SECOND = 5
FIELDS = ("q", "g", "d", "s")


def swap_pairs(n_lon, n_lat):
    half = n_lon // 2

    def flat(move):
        pairs = []
        for i in range(n_lon):
            for j in range(n_lat):
                k, m = move(i, j)
                pairs.append((i * n_lat + j, k * n_lat + m))
        return pairs

    def lat_odd(i, j):
        if j == 0 or j == n_lat - 1:
            return (i + half) % n_lon, j
        return i, ((j + 1) ^ 1) - 1

    return {
        "lon_even": flat(lambda i, j: (i ^ 1, j)),
        "lon_odd": flat(lambda i, j: ((((i + 1) ^ 1) - 1) % n_lon, j)),
        "lat_even": flat(lambda i, j: (i, j ^ 1)),
        "lat_odd": flat(lat_odd),
    }


def plus(a, b):
    if a is None or b is None:
        return b if a is None else a
    return a + b


def times(a, b):
    return None if a is None or b is None else a * b


def add_scaled(a, scale, b):
    size = max(len(a), len(b))
    a, b = (list(v) + [None] * (size - len(v)) for v in (a, b))
    return [plus(x, times(scale, y)) for x, y in zip(a, b)]


def krylov_coefficients(first, mixed, rest, shift, one):
    def inner(a, b):
        total = times(times(a[0], b[0]), first)
        for x, others in ((a[0], b), (b[0], a)):
            for j in range(1, len(others)):
                total = plus(total, times(times(x, others[j]), mixed[j - 1]))
        for k in range(len(a) + len(b) - 3):
            part = None
            for i in range(1, len(a)):
                if 1 <= k + 2 - i < len(b):
                    part = plus(part, times(a[i], b[k + 2 - i]))
            total = plus(total, times(part, rest[k]))
        return total

    def image_of(a):
        return [None] + [plus(v, times(shift, a[k + 1]) if k + 1 < len(a) else None) for k, v in enumerate(a)]

    shadow = [one]
    residual = [one]
    direction = [one]
    solution = []
    rho = first
    for iteration in range(ITERS):
        image = image_of(direction)
        alpha = rho / inner(shadow, image)
        half = add_scaled(residual, -alpha, image)
        second = image_of(half)
        omega = inner(second, half) / inner(second, second)
        solution = add_scaled(solution, alpha, direction)
        solution = add_scaled(solution, omega, half)
        residual = add_scaled(half, -omega, second)
        if iteration + 1 < ITERS:
            rho_next = inner(shadow, half) - omega * inner(shadow, second)
            beta = rho_next / rho * (alpha / omega)
            direction = add_scaled(residual, beta, add_scaled(direction, -omega, image))
            rho = rho_next
    return solution, residual


PAIRS = (
    [(0, j) for j in range(2 * ITERS + 1)]
    + [(1 + k // 2, 1 + k - k // 2) for k in range(4 * ITERS - 1)]
)


def lanes_of(levels):
    return lax.broadcasted_iota(jnp.int32, (levels, LANES), 1)


def turn(value, shift):
    shift %= LANES
    return value if shift == 0 else pltpu.roll(value, shift, 1)


def plane(ref, column, columns, levels, shift=0):
    return ref.at[pl.ds((1 + shift) * columns + column, levels, stride=columns), :]


def clear_ends(ref, columns, levels):
    ref[0:columns, :] = jnp.zeros((columns, LANES), jnp.float32)
    ref[(levels + 1) * columns : (levels + 2) * columns, :] = jnp.zeros((columns, LANES), jnp.float32)


def column(ref, i, own, levels):
    return ref[pl.ds(i, levels, stride=own), :]


def shifted_rows(main, strip, lane, strips=True):
    main_s, main_n = turn(main, -1), turn(main, 1)
    strip_s, strip_n = turn(strip, -1), turn(strip, 1)
    first, last = lane == 0, lane == LANES - 1
    out = [jnp.where(last, strip_s, main_s) + jnp.where(first, strip_n, main_n)]
    if strips:
        out.append(jnp.where(last, main_s, strip_s) + jnp.where(first, main_n, strip_n))
    return out


def transformed(x, b, c, h, above, below):
    return {"q": c * x, "g": c * c, "d": (4.0 + h) + (above + below), "s": c * b}


def parity(size):
    i, j = lax.axis_index("lon"), lax.axis_index("lat")
    pole = (j == 0) | (j == size - 1)
    return 1 - lax.rem(i, 2), 1 - lax.rem(j, 2), pole


def pack_kernel(own, levels, n_lat, x_hbm, b_hbm, c_hbm, h_hbm, coupling_hbm, to_a, to_b, lat_a, lat_b, above,
                below, fq, fg, fd, fs, x, b, c, h, coupling, q_ref, partial, sem):
    copies = []
    moves = ((coupling_hbm, coupling), (x_hbm, x), (c_hbm, c), (h_hbm, h), (b_hbm, b))
    for k, (source, target) in enumerate(moves):
        copies.append(pltpu.make_async_copy(source, target, sem.at[k]))
        copies[-1].start()
    lane = lanes_of(levels)
    group = lane // GROUP
    groups = LANES // GROUP
    lon_even, lat_even, pole = parity(n_lat)
    store = dict(zip(FIELDS, (fq, fg, fd, fs)))
    copies[0].wait()
    wide = (levels, levels - 1)
    row, interface = (lax.broadcasted_iota(jnp.int32, wide, k) for k in (0, 1))
    strength = jnp.broadcast_to(coupling[...], wide)
    for out, k in ((below, row), (above, row - 1)):
        value = jnp.sum(jnp.where(interface == k, strength, 0.0), axis=1, keepdims=True)
        out[...] = jnp.broadcast_to(value, (levels, LANES))
    north = jnp.zeros((levels, LANES), jnp.float32)
    south = north
    for copy in copies[1:]:
        copy.wait()
    for i in range(own):
        values = transformed(
            column(x, i, own, levels),
            column(b, i, own, levels),
            column(c, i, own, levels),
            column(h, i, own, levels),
            above[...],
            below[...],
        )
        for f, name in enumerate(FIELDS):
            store[name][pl.ds(i, levels, stride=own), :] = values[name]
            if name == "q":
                plane(q_ref, i, own, levels)[...] = values[name]
            slot = f * own + i
            rolled = turn(values[name], GROUP * slot)
            north = jnp.where(group == slot, rolled, north)
            south = jnp.where(group == (slot - 1) % groups, rolled, south)
    even = jnp.full((levels, LANES), lat_even, jnp.int32) == 1
    over = jnp.full((levels, LANES), pole.astype(jnp.int32), jnp.int32) == 1
    lat_a[...] = jnp.where(even, south, north)
    other = jnp.where(even, north, south)
    mirror = other
    for bit in (1, 2, 4):
        mirror = jnp.where((lane & bit) != 0, turn(mirror, bit), turn(mirror, -bit))
    mirror = jnp.where(even, turn(mirror, -GROUP), turn(mirror, GROUP))
    lat_b[...] = jnp.where(over, mirror, other)
    clear_ends(q_ref, own, levels)
    for k, (i, inner) in enumerate(((0, 1), (own - 1, own - 2))):
        q = plane(q_ref, i, own, levels)[...]
        near = jnp.where(lane == LANES - 1, 0.0, turn(q, -1)) + jnp.where(lane == 0, 0.0, turn(q, 1))
        near = near + plane(q_ref, inner, own, levels)[...]
        near = near + below[...] * plane(q_ref, i, own, levels, 1)[...]
        near = near + above[...] * plane(q_ref, i, own, levels, -1)[...]
        image = column(fd, i, own, levels) * q - near
        partial[k] = column(fs, i, own, levels) - column(fg, i, own, levels) * image
    for message, side in ((to_a, lon_even), (to_b, 1 - lon_even)):
        i = jnp.where(side == 1, own - 1, 0)
        message[0] = column(fq, i, own, levels)
        message[1] = partial[side]
        message[2] = column(fg, i, own, levels)


def corner_kernel(own, levels, n_lat, lat_a, lat_b, to_a, to_b):
    lane = lanes_of(levels)
    quarter = (lane // GROUP) % own
    lon_even, lat_even, _ = parity(n_lat)
    even = jnp.full((levels, LANES), lat_even, jnp.int32) == 1
    lon = jnp.full((levels, LANES), lon_even, jnp.int32) == 1
    a, b = lat_a[...], lat_b[...]
    north, south = jnp.where(even, b, a), jnp.where(even, a, b)
    east = jnp.where(quarter >= own - NEAR, south, turn(north, GROUP * (1 - NEAR)))
    west = jnp.where(quarter < NEAR, south, turn(north, GROUP * (1 + NEAR)))
    to_a[...] = jnp.where(lon, east, west)
    to_b[...] = jnp.where(lon, west, east)


def lane_value(row, k):
    lane = lax.broadcasted_iota(jnp.int32, (1, LANES), 1)
    return jnp.sum(jnp.where(lane == k, row, 0.0), axis=1, keepdims=True)


def put_row(out, arrays):
    lane = lax.broadcasted_iota(jnp.int32, (1, LANES), 1)
    row = jnp.zeros((1, LANES), jnp.float32)
    for k, value in enumerate(arrays):
        row = jnp.where(lane == k, value.total(), row)
    out[...] = jnp.broadcast_to(row[None], out.shape)


def total_row(gathered):
    return jnp.sum(gathered[...], axis=0)


class Extended:
    def __init__(self, columns, levels, d, g, above, below, far=None):
        self.columns, self.levels = columns, levels
        self.d, self.g = d, g
        self.above, self.below = above, below
        self.far = far

    def at(self, pair, k, e, rows, shift=0):
        start, count = rows
        return pair[k][pl.ds((1 + start + shift) * self.columns + e, count, stride=self.columns), :]

    def set(self, pair, k, e, rows, value):
        start, count = rows
        pair[k][pl.ds((1 + start) * self.columns + e, count, stride=self.columns), :] = value

    def put(self, pair, k, e, value):
        self.set(pair, k, e, (0, self.levels), value)

    def diagonal(self, k, e, rows):
        edges = (FAR - 1, self.columns - FAR)
        if self.far is not None and k == 0 and e in edges:
            start, count = rows
            return self.far[edges.index(e), start : start + count, :]
        return self.at(self.d, k, e, rows)

    def sweep(self, pair, first, last, strips=True):
        for start in range(0, self.levels, SUBLANES):
            rows = start, min(SUBLANES, self.levels - start)
            lane = lanes_of(rows[1])
            above, below = (ref[start : start + rows[1], :] for ref in (self.above, self.below))
            center = {}

            def middle(k, e):
                if (k, e) not in center:
                    center[k, e] = self.at(pair, k, e, rows)
                return center[k, e]

            for e in range(first, last + 1):
                near = shifted_rows(middle(0, e), middle(1, e), lane, strips)
                out = []
                for k in range(1 + strips):
                    q = middle(k, e)
                    side = middle(k, e - 1) + middle(k, e + 1)
                    levels = below * self.at(pair, k, e, rows, 1) + above * self.at(pair, k, e, rows, -1)
                    out.append((q, self.diagonal(k, e, rows) * q - (side + near[k]) - levels))
                yield rows, e, out


class Sums:
    def __init__(self):
        self.parts = {}

    def add(self, value):
        count = value.shape[0]
        self.parts[count] = self.parts[count] + value if count in self.parts else value

    def total(self):
        return sum(jnp.sum(v, keepdims=True) for v in self.parts.values())


def own_rows(i, own, rows):
    start, count = rows
    return pl.ds(start * own + i, count, stride=own), slice(None)


def own_kernel(own, levels, columns, n_lat, fq, fg, fd, fs, lat_a, lat_b, *outs):
    group = lanes_of(levels) // GROUP
    _, lat_even, _ = parity(n_lat)
    even = jnp.full((levels, LANES), lat_even, jnp.int32) == 1
    a, b = lat_a[...], lat_b[...]
    north, south = jnp.where(even, b, a), jnp.where(even, a, b)
    for f, field in enumerate((fq, fg, fd, fs)):
        main, strip = outs[2 * f : 2 * f + 2]
        if f == 0:
            clear_ends(main, columns, levels)
            clear_ends(strip, columns, levels)
        for i in range(own):
            slot = f * own + i
            plane(main, FAR + i, columns, levels)[...] = column(field, i, own, levels)
            edges = turn(jnp.where(group == slot, south, north), -GROUP * slot)
            plane(strip, FAR + i, columns, levels)[...] = edges


def first_kernel(own, levels, columns, n_lat, fd, above, below, from_a, from_b, corners_a, corners_b, *refs):
    extended = refs[8:16]
    k0, k1, k1_strip, to_a, to_b, out, qb_main, qb_strip = refs[16:]
    lane = lanes_of(levels)
    low = lane < LANES // 2
    lon_even, _, _ = parity(n_lat)
    pairs = {name: extended[2 * f : 2 * f + 2] for f, name in enumerate(FIELDS)}
    qa, qb = pairs["q"], (qb_main, qb_strip)
    ext = Extended(columns, levels, pairs["d"], pairs["g"], above, below)
    for ref in qb:
        clear_ends(ref, columns, levels)
    for block, corner, east in ((from_a, corners_a, lon_even), (from_b, corners_b, 1 - lon_even)):
        tile = corner[...]
        for k, name in enumerate(FIRST):
            ext.put(pairs[name], 0, jnp.where(east == 1, FAR + own, FAR - 1), block[k])
        for name, distance in STRIPS:
            e = jnp.where(east == 1, FAR + own - 1 + distance, FAR - distance)
            slot = FIELDS.index(name) * own + jnp.where(east == 1, distance - 1, own - distance)
            south = lax.rem(2 * LANES - GROUP * slot, LANES)
            north = lax.rem(south + LANES - GROUP * jnp.where(east == 1, 1 + NEAR, 1 - NEAR), LANES)
            ext.put(pairs[name], 1, e, jnp.where(low, pltpu.roll(tile, south, 1), pltpu.roll(tile, north, 1)))
    edges = {FAR - 1: FAR, FAR + own: FAR + own - 1}
    for rows, e, tiles in ext.sweep(qa, FAR - 1, FAR + own):
        for k, (_, image) in enumerate(tiles):
            if k == 0 and e in edges:
                edge, strip = ext.at(qa, 0, edges[e], rows), ext.at(qa, 1, e, rows)
                place = lanes_of(rows[1])
                beyond = jnp.where(place == LANES - 1, turn(strip, -1), 0.0) + jnp.where(
                    place == 0, turn(strip, 1), 0.0
                )
                image = -(edge + beyond)
            value = ext.at(pairs["s"], k, e, rows) - ext.at(pairs["g"], k, e, rows) * image
            ext.set(qb, k, e, rows, value)
            if k == 0 and FAR <= e < FAR + own:
                k0[own_rows(e - FAR, own, rows)] = value
    mixed, square = Sums(), Sums()
    for rows, e, tiles in ext.sweep(qb, FAR, FAR + own - 1):
        for k, (q, image) in enumerate(tiles):
            value = ext.at(pairs["g"], k, e, rows) * image
            (k1, k1_strip)[k][own_rows(e - FAR, own, rows)] = value
            ext.set(qa, k, e, rows, value)
            if k == 0:
                mixed.add(q * image)
                square.add(value * image)
    put_row(out, (mixed, square))
    for rows, e, tiles in ext.sweep(qa, FAR + NEAR - 1, FAR + own - NEAR):
        for k, (_, image) in enumerate(tiles):
            ext.set(qb, k, e, rows, ext.at(pairs["g"], k, e, rows) * image)
    for message, side in ((to_a, lon_even), (to_b, 1 - lon_even)):
        near, next_one = (jnp.where(side == 1, own - d, d - 1) for d in (1, NEAR))
        packed = jnp.zeros((levels, LANES), jnp.float32)
        for k, (main, strip) in enumerate(
            (
                (column(k1, near, own, levels), column(k1_strip, near, own, levels)),
                (column(k1, next_one, own, levels), column(k1_strip, next_one, own, levels)),
                [plane(ref, FAR + next_one, columns, levels)[...] for ref in qb],
            )
        ):
            message[k] = main
            rolled = turn(strip, 2 * GROUP * k + GROUP)
            packed = jnp.where(lane // (2 * GROUP) == k, rolled, packed)
        message[SECOND - 2] = packed
        message[SECOND - 1] = column(fd, near, own, levels)


def second_kernel(own, levels, columns, n_lat, k0, k1, k1_strip, from_a, from_b, g_main, g_strip, d_main, d_strip,
                  above, below, shift_sums, k2, k3, k4, out, shift_row, qa_main, qa_strip, qb_main, qb_strip, far):
    lon_even, _, _ = parity(n_lat)
    qa, qb = (qa_main, qa_strip), (qb_main, qb_strip)
    g = (g_main, g_strip)
    ext = Extended(columns, levels, (d_main, d_strip), g, above, below, far)
    for ref in (*qa, *qb):
        clear_ends(ref, columns, levels)
    row = total_row(shift_sums)
    mixed, square = lane_value(row, 0), lane_value(row, 1)
    shift = jnp.where(mixed > 0.0, square / jnp.where(mixed > 0.0, mixed, 1.0), 1.0)
    shift_row[...] = jnp.broadcast_to(shift, shift_row.shape)
    shift = jnp.broadcast_to(shift, (levels, LANES))
    for i in range(own):
        ext.put(qa, 0, FAR + i, column(k1, i, own, levels))
        ext.put(qa, 1, FAR + i, column(k1_strip, i, own, levels))
    for block, east in ((from_a, lon_even), (from_b, 1 - lon_even)):
        strips = [turn(block[SECOND - 2], -(2 * GROUP * k + GROUP)) for k in range(3)]
        near, next_one = (jnp.where(east == 1, FAR + own - 1 + d, FAR - d) for d in (1, NEAR))
        for k in range(2):
            first, other, image = ((block[d], strips[d])[k] for d in range(3))
            ext.put(qa, k, near, first)
            ext.put(qa, k, next_one, other)
            ext.put(qb, k, next_one, image - shift * other)
        far[east] = block[SECOND - 1]
    shift = shift[:SUBLANES]
    for rows, e, tiles in ext.sweep(qa, FAR - 1, FAR + own):
        for k, (q, image) in enumerate(tiles):
            value = ext.at(g, k, e, rows) * image - shift[: rows[1]] * q
            ext.set(qb, k, e, rows, value)
            if k == 0 and FAR <= e < FAR + own:
                k2[own_rows(e - FAR, own, rows)] = value
    for rows, e, tiles in ext.sweep(qb, FAR - 1, FAR + own):
        for k, (q, image) in enumerate(tiles):
            value = ext.at(g, k, e, rows) * image - shift[: rows[1]] * q
            ext.set(qa, k, e, rows, value)
            if k == 0 and FAR <= e < FAR + own:
                k3[own_rows(e - FAR, own, rows)] = value
    sums = [Sums() for _ in PAIRS]
    for rows, e, ((q, image),) in ext.sweep(qa, FAR, FAR + own - 1, strips=False):
        place = own_rows(e - FAR, own, rows)
        scale = ext.at(g, 0, e, rows)
        last = scale * image - shift[: rows[1]] * q
        k4[place] = last
        v = [k0[place], k1[place], k2[place], q, last]
        w = 1.0 / scale
        lead = [a * w for a in v]
        for total, (a, b) in zip(sums, PAIRS):
            total.add(lead[a] * v[b])
    put_row(out, sums)


def final_kernel(sums, shift_row, x, c, k0, k1, k2, k3, k4, out, rest):
    row = total_row(sums)
    first, *others = [lane_value(row, k) for k in range(len(PAIRS))]
    shift = lane_value(shift_row[...], 0)
    one = jnp.ones((1, 1), jnp.float32)
    solution, residual = krylov_coefficients(first, others[: 2 * ITERS], others[2 * ITERS :], shift, one)
    vectors = (k0, k1, k2, k3, k4)
    inverse = 1.0 / c[...]

    def combined(coefficients):
        total = None
        for a, v in zip(coefficients, vectors):
            term = a * v[...]
            total = term if total is None else total + term
        return total * inverse

    out[...] = x[...] + combined(solution)
    rest[...] = combined(residual)


def program(right_side, first_guess, cell_scale, helmholtz_term, vertical_coupling):
    n_lon, n_lat = lax.axis_size("lon"), lax.axis_size("lat")
    levels, own, width = right_side.shape
    assert width == LANES and own == 2 * NEAR >= FAR and len(FIELDS) * own * GROUP == LANES
    assert n_lon % 4 == 0 and n_lat % 2 == 0
    columns = own + 2 * FAR
    pairs = swap_pairs(n_lon, n_lat)
    coupling = vertical_coupling.reshape(1, levels - 1)
    b, x, c, h = (v.reshape(levels * own, LANES) for v in (right_side, first_guess, cell_scale, helmholtz_term))

    def real(*shape):
        return jax.ShapeDtypeStruct(shape, jnp.float32)

    def call(kernel, ins, outs, scratch=(), specs=None, aliases=()):
        return pl.pallas_call(
            kernel,
            out_shape=tuple(outs) if len(outs) > 1 else outs[0],
            in_specs=specs or [VMEM] * len(ins),
            out_specs=tuple([VMEM] * len(outs)) if len(outs) > 1 else VMEM,
            scratch_shapes=[pltpu.VMEM(s, jnp.float32) if isinstance(s, tuple) else s for s in scratch],
            compiler_params=pltpu.CompilerParams(vmem_limit_bytes=32 * 1024 * 1024),
            input_output_aliases=dict(aliases),
        )(*ins)

    def swap(value, name):
        return lax.ppermute(value, AXES, pairs[name])

    def everywhere(rows):
        return lax.all_to_all(rows, AXES, 0, 0, tiled=True)

    whole = real(levels * own, LANES)
    tile = real(levels, LANES)
    rows = real(n_lon * n_lat, 1, LANES)
    extended = ((levels + 2) * columns, LANES)

    to_a, to_b, lat_a, lat_b, above, below, *fields = call(
        functools.partial(pack_kernel, own, levels, n_lat),
        tuple(pltpu.with_memory_space_constraint(v, pltpu.HBM) for v in (x, b, c, h, coupling)),
        [real(len(FIRST), levels, LANES)] * 2 + [tile] * 4 + [whole] * len(FIELDS),
        [(levels * own, LANES)] * 4
        + [(1, levels - 1), ((levels + 2) * own, LANES), (2, levels, LANES), pltpu.SemaphoreType.DMA((5,))],
        [pl.BlockSpec(memory_space=pltpu.HBM)] * 5,
    )
    lat_a = swap(lat_a, "lat_even")
    lat_b = swap(lat_b, "lat_odd")
    from_a = swap(to_a, "lon_even")
    from_b = swap(to_b, "lon_odd")
    corners_a, corners_b = call(
        functools.partial(corner_kernel, own, levels, n_lat), (lat_a, lat_b), [tile] * 2
    )
    corners_a = swap(corners_a, "lon_even")
    corners_b = swap(corners_b, "lon_odd")
    buffers = call(
        functools.partial(own_kernel, own, levels, columns, n_lat),
        (*fields, lat_a, lat_b),
        [real(*extended)] * 2 * len(FIELDS),
    )
    ins = (fields[2], above, below, from_a, from_b, corners_a, corners_b, *buffers)
    *buffers, k0, k1, k1_strip, to_a, to_b, shift_sums = call(
        functools.partial(first_kernel, own, levels, columns, n_lat),
        ins,
        [real(*extended)] * 2 * len(FIELDS)
        + [whole] * 3
        + [real(SECOND, levels, LANES)] * 2
        + [rows],
        [extended] * 2,
        aliases=[(len(ins) - 2 * len(FIELDS) + k, k) for k in range(2 * len(FIELDS))],
    )
    coefficients = buffers[2:6]
    from_a = swap(to_a, "lon_even")
    from_b = swap(to_b, "lon_odd")
    shift_sums = everywhere(shift_sums)
    k2, k3, k4, sums, shift = call(
        functools.partial(second_kernel, own, levels, columns, n_lat),
        (k0, k1, k1_strip, from_a, from_b, *coefficients, above, below, shift_sums),
        [whole] * 3 + [rows, real(1, LANES)],
        [extended] * 4 + [(2, levels, LANES)],
    )
    sums = everywhere(sums)
    out, rest = call(final_kernel, (sums, shift, x, c, k0, k1, k2, k3, k4), [whole] * 2)
    return out.reshape(right_side.shape), rest.reshape(right_side.shape)


def solution(mesh):
    spec = P(None, "lon", "lat")
    return jax.shard_map(
        program, mesh=mesh, in_specs=(spec, spec, spec, spec, P()), out_specs=(spec, spec), check_vma=False
    )
```

```python
import functools

import jax
import jax.numpy as jnp
from jax import lax
from jax.experimental import pallas as pl
from jax.experimental.pallas import tpu as pltpu
from jax.sharding import PartitionSpec as P


AXES = ("lon", "lat")
ITERS = 2
LANES = 128
SUBLANES = 8
NEAR, FAR = 2, 3
GROUP = 8
VMEM = pl.BlockSpec(memory_space=pltpu.VMEM)
FIRST = ("q", "s", "g")
STRIPS = (("q", 1), ("q", 2), ("g", 1), ("d", 1), ("s", 1))
SECOND = 5
FIELDS = ("q", "g", "d", "s")


def swap_pairs(n_lon, n_lat):
    half = n_lon // 2

    def flat(move):
        pairs = []
        for i in range(n_lon):
            for j in range(n_lat):
                k, m = move(i, j)
                pairs.append((i * n_lat + j, k * n_lat + m))
        return pairs

    def lat_odd(i, j):
        if j == 0 or j == n_lat - 1:
            return (i + half) % n_lon, j
        return i, ((j + 1) ^ 1) - 1

    return {
        "lon_even": flat(lambda i, j: (i ^ 1, j)),
        "lon_odd": flat(lambda i, j: ((((i + 1) ^ 1) - 1) % n_lon, j)),
        "lat_even": flat(lambda i, j: (i, j ^ 1)),
        "lat_odd": flat(lat_odd),
    }


def plus(a, b):
    if a is None or b is None:
        return b if a is None else a
    return a + b


def times(a, b):
    return None if a is None or b is None else a * b


def add_scaled(a, scale, b):
    size = max(len(a), len(b))
    a, b = (list(v) + [None] * (size - len(v)) for v in (a, b))
    return [plus(x, times(scale, y)) for x, y in zip(a, b)]


def krylov_coefficients(first, mixed, rest, shift, one):
    def inner(a, b):
        total = times(times(a[0], b[0]), first)
        for x, others in ((a[0], b), (b[0], a)):
            for j in range(1, len(others)):
                total = plus(total, times(times(x, others[j]), mixed[j - 1]))
        for k in range(len(a) + len(b) - 3):
            part = None
            for i in range(1, len(a)):
                if 1 <= k + 2 - i < len(b):
                    part = plus(part, times(a[i], b[k + 2 - i]))
            total = plus(total, times(part, rest[k]))
        return total

    def image_of(a):
        return [None] + [plus(v, times(shift, a[k + 1]) if k + 1 < len(a) else None) for k, v in enumerate(a)]

    shadow = [one]
    residual = [one]
    direction = [one]
    solution = []
    rho = first
    for iteration in range(ITERS):
        image = image_of(direction)
        alpha = rho / inner(shadow, image)
        half = add_scaled(residual, -alpha, image)
        second = image_of(half)
        omega = inner(second, half) / inner(second, second)
        solution = add_scaled(solution, alpha, direction)
        solution = add_scaled(solution, omega, half)
        residual = add_scaled(half, -omega, second)
        if iteration + 1 < ITERS:
            rho_next = inner(shadow, half) - omega * inner(shadow, second)
            beta = rho_next / rho * (alpha / omega)
            direction = add_scaled(residual, beta, add_scaled(direction, -omega, image))
            rho = rho_next
    return solution, residual


PAIRS = (
    [(0, j) for j in range(2 * ITERS + 1)]
    + [(1 + k // 2, 1 + k - k // 2) for k in range(4 * ITERS - 1)]
)


def lanes_of(levels):
    return lax.broadcasted_iota(jnp.int32, (levels, LANES), 1)


def turn(value, shift):
    shift %= LANES
    return value if shift == 0 else pltpu.roll(value, shift, 1)


def plane(ref, column, columns, levels, shift=0):
    return ref.at[pl.ds((1 + shift) * columns + column, levels, stride=columns), :]


def clear_ends(ref, columns, levels):
    ref[0:columns, :] = jnp.zeros((columns, LANES), jnp.float32)
    ref[(levels + 1) * columns : (levels + 2) * columns, :] = jnp.zeros((columns, LANES), jnp.float32)


def column(ref, i, own, levels):
    return ref[pl.ds(i, levels, stride=own), :]


def shifted_rows(main, strip, lane, strips=True):
    main_s, main_n = turn(main, -1), turn(main, 1)
    strip_s, strip_n = turn(strip, -1), turn(strip, 1)
    first, last = lane == 0, lane == LANES - 1
    out = [jnp.where(last, strip_s, main_s) + jnp.where(first, strip_n, main_n)]
    if strips:
        out.append(jnp.where(last, main_s, strip_s) + jnp.where(first, main_n, strip_n))
    return out


def transformed(x, b, c, h, above, below):
    return {"q": c * x, "g": c * c, "d": (4.0 + h) + (above + below), "s": c * b}


def parity(size):
    i, j = lax.axis_index("lon"), lax.axis_index("lat")
    pole = (j == 0) | (j == size - 1)
    return 1 - lax.rem(i, 2), 1 - lax.rem(j, 2), pole


def pack_kernel(own, levels, n_lat, x_hbm, b_hbm, c_hbm, h_hbm, coupling_hbm, to_a, to_b, lat_a, lat_b, above,
                below, fq, fg, fd, fs, x, b, c, h, coupling, q_ref, partial, sem):
    copies = []
    moves = ((coupling_hbm, coupling), (x_hbm, x), (c_hbm, c), (h_hbm, h), (b_hbm, b))
    for k, (source, target) in enumerate(moves):
        copies.append(pltpu.make_async_copy(source, target, sem.at[k]))
        copies[-1].start()
    lane = lanes_of(levels)
    groups = LANES // GROUP
    lon_even, lat_even, pole = parity(n_lat)
    store = dict(zip(FIELDS, (fq, fg, fd, fs)))
    copies[0].wait()
    wide = (levels, levels - 1)
    row, interface = (lax.broadcasted_iota(jnp.int32, wide, k) for k in (0, 1))
    strength = jnp.broadcast_to(coupling[...], wide)
    for out, k in ((below, row), (above, row - 1)):
        value = jnp.sum(jnp.where(interface == k, strength, 0.0), axis=1, keepdims=True)
        out[...] = jnp.broadcast_to(value, (levels, LANES))
    for copy in copies[1:]:
        copy.wait()
    for start in range(0, levels, SUBLANES):
        rows = start, min(SUBLANES, levels - start)
        block, shape = slice(start, start + rows[1]), (rows[1], LANES)
        row_lane = lanes_of(rows[1])
        group = row_lane // GROUP
        north = jnp.zeros(shape, jnp.float32)
        south = north
        for i in range(own):
            place = own_rows(i, own, rows)
            values = transformed(x[place], b[place], c[place], h[place], above[block, :], below[block, :])
            for f, name in enumerate(FIELDS):
                store[name][place] = values[name]
                if name == "q":
                    q_ref[pl.ds((1 + start) * own + i, rows[1], stride=own), :] = values[name]
                slot = f * own + i
                rolled = turn(values[name], GROUP * slot)
                north = jnp.where(group == slot, rolled, north)
                south = jnp.where(group == (slot - 1) % groups, rolled, south)
        even = jnp.full(shape, lat_even, jnp.int32) == 1
        over = jnp.full(shape, pole.astype(jnp.int32), jnp.int32) == 1
        lat_a[block, :] = jnp.where(even, south, north)
        other = jnp.where(even, north, south)
        mirror = other
        for bit in (1, 2, 4):
            mirror = jnp.where((row_lane & bit) != 0, turn(mirror, bit), turn(mirror, -bit))
        mirror = jnp.where(even, turn(mirror, -GROUP), turn(mirror, GROUP))
        lat_b[block, :] = jnp.where(over, mirror, other)
    clear_ends(q_ref, own, levels)
    for k, (i, inner) in enumerate(((0, 1), (own - 1, own - 2))):
        q = plane(q_ref, i, own, levels)[...]
        near = jnp.where(lane == LANES - 1, 0.0, turn(q, -1)) + jnp.where(lane == 0, 0.0, turn(q, 1))
        near = near + plane(q_ref, inner, own, levels)[...]
        near = near + below[...] * plane(q_ref, i, own, levels, 1)[...]
        near = near + above[...] * plane(q_ref, i, own, levels, -1)[...]
        image = column(fd, i, own, levels) * q - near
        partial[k] = column(fs, i, own, levels) - column(fg, i, own, levels) * image
    for message, side in ((to_a, lon_even), (to_b, 1 - lon_even)):
        i = jnp.where(side == 1, own - 1, 0)
        message[0] = column(fq, i, own, levels)
        message[1] = partial[side]
        message[2] = column(fg, i, own, levels)


def corner_kernel(own, levels, n_lat, lat_a, lat_b, to_a, to_b):
    lane = lanes_of(levels)
    quarter = (lane // GROUP) % own
    lon_even, lat_even, _ = parity(n_lat)
    even = jnp.full((levels, LANES), lat_even, jnp.int32) == 1
    lon = jnp.full((levels, LANES), lon_even, jnp.int32) == 1
    a, b = lat_a[...], lat_b[...]
    north, south = jnp.where(even, b, a), jnp.where(even, a, b)
    east = jnp.where(quarter >= own - NEAR, south, turn(north, GROUP * (1 - NEAR)))
    west = jnp.where(quarter < NEAR, south, turn(north, GROUP * (1 + NEAR)))
    to_a[...] = jnp.where(lon, east, west)
    to_b[...] = jnp.where(lon, west, east)


def lane_value(row, k):
    lane = lax.broadcasted_iota(jnp.int32, (1, LANES), 1)
    return jnp.sum(jnp.where(lane == k, row, 0.0), axis=1, keepdims=True)


def put_row(out, arrays):
    lane = lax.broadcasted_iota(jnp.int32, (1, LANES), 1)
    row = jnp.zeros((1, LANES), jnp.float32)
    for k, value in enumerate(arrays):
        row = jnp.where(lane == k, value.total(), row)
    out[...] = jnp.broadcast_to(row[None], out.shape)


def total_row(gathered):
    return jnp.sum(gathered[...], axis=0)


class Extended:
    def __init__(self, columns, levels, d, g, above, below, far=None):
        self.columns, self.levels = columns, levels
        self.d, self.g = d, g
        self.above, self.below = above, below
        self.far = far

    def at(self, pair, k, e, rows, shift=0):
        start, count = rows
        return pair[k][pl.ds((1 + start + shift) * self.columns + e, count, stride=self.columns), :]

    def set(self, pair, k, e, rows, value):
        start, count = rows
        pair[k][pl.ds((1 + start) * self.columns + e, count, stride=self.columns), :] = value

    def put(self, pair, k, e, value):
        self.set(pair, k, e, (0, self.levels), value)

    def diagonal(self, k, e, rows):
        edges = (FAR - 1, self.columns - FAR)
        if self.far is not None and k == 0 and e in edges:
            start, count = rows
            return self.far[edges.index(e), start : start + count, :]
        return self.at(self.d, k, e, rows)

    def sweep(self, pair, first, last, strips=True):
        for start in range(0, self.levels, SUBLANES):
            rows = start, min(SUBLANES, self.levels - start)
            lane = lanes_of(rows[1])
            above, below = (ref[start : start + rows[1], :] for ref in (self.above, self.below))
            center = {}

            def middle(k, e):
                if (k, e) not in center:
                    center[k, e] = self.at(pair, k, e, rows)
                return center[k, e]

            for e in range(first, last + 1):
                near = shifted_rows(middle(0, e), middle(1, e), lane, strips)
                out = []
                for k in range(1 + strips):
                    q = middle(k, e)
                    side = middle(k, e - 1) + middle(k, e + 1)
                    levels = below * self.at(pair, k, e, rows, 1) + above * self.at(pair, k, e, rows, -1)
                    out.append((q, self.diagonal(k, e, rows) * q - (side + near[k]) - levels))
                yield rows, e, out


class Sums:
    def __init__(self):
        self.parts = {}

    def add(self, value):
        count = value.shape[0]
        self.parts[count] = self.parts[count] + value if count in self.parts else value

    def total(self):
        return sum(jnp.sum(v, keepdims=True) for v in self.parts.values())


def own_rows(i, own, rows):
    start, count = rows
    return pl.ds(start * own + i, count, stride=own), slice(None)


def own_kernel(own, levels, columns, n_lat, fq, fg, fd, fs, lat_a, lat_b, *outs):
    group = lanes_of(levels) // GROUP
    _, lat_even, _ = parity(n_lat)
    even = jnp.full((levels, LANES), lat_even, jnp.int32) == 1
    a, b = lat_a[...], lat_b[...]
    north, south = jnp.where(even, b, a), jnp.where(even, a, b)
    for f, field in enumerate((fq, fg, fd, fs)):
        main, strip = outs[2 * f : 2 * f + 2]
        if f == 0:
            clear_ends(main, columns, levels)
            clear_ends(strip, columns, levels)
        for i in range(own):
            slot = f * own + i
            plane(main, FAR + i, columns, levels)[...] = column(field, i, own, levels)
            edges = turn(jnp.where(group == slot, south, north), -GROUP * slot)
            plane(strip, FAR + i, columns, levels)[...] = edges


def first_kernel(own, levels, columns, n_lat, fd, above, below, from_a, from_b, corners_a, corners_b, *refs):
    extended = refs[8:16]
    k0, k1, k1_strip, to_a, to_b, out, qb_main, qb_strip = refs[16:]
    lane = lanes_of(levels)
    low = lane < LANES // 2
    lon_even, _, _ = parity(n_lat)
    pairs = {name: extended[2 * f : 2 * f + 2] for f, name in enumerate(FIELDS)}
    qa, qb = pairs["q"], (qb_main, qb_strip)
    ext = Extended(columns, levels, pairs["d"], pairs["g"], above, below)
    for ref in qb:
        clear_ends(ref, columns, levels)
    for block, corner, east in ((from_a, corners_a, lon_even), (from_b, corners_b, 1 - lon_even)):
        tile = corner[...]
        for k, name in enumerate(FIRST):
            ext.put(pairs[name], 0, jnp.where(east == 1, FAR + own, FAR - 1), block[k])
        for name, distance in STRIPS:
            e = jnp.where(east == 1, FAR + own - 1 + distance, FAR - distance)
            slot = FIELDS.index(name) * own + jnp.where(east == 1, distance - 1, own - distance)
            south = lax.rem(2 * LANES - GROUP * slot, LANES)
            north = lax.rem(south + LANES - GROUP * jnp.where(east == 1, 1 + NEAR, 1 - NEAR), LANES)
            ext.put(pairs[name], 1, e, jnp.where(low, pltpu.roll(tile, south, 1), pltpu.roll(tile, north, 1)))
    edges = {FAR - 1: FAR, FAR + own: FAR + own - 1}
    for rows, e, tiles in ext.sweep(qa, FAR - 1, FAR + own):
        for k, (_, image) in enumerate(tiles):
            if k == 0 and e in edges:
                edge, strip = ext.at(qa, 0, edges[e], rows), ext.at(qa, 1, e, rows)
                place = lanes_of(rows[1])
                beyond = jnp.where(place == LANES - 1, turn(strip, -1), 0.0) + jnp.where(
                    place == 0, turn(strip, 1), 0.0
                )
                image = -(edge + beyond)
            value = ext.at(pairs["s"], k, e, rows) - ext.at(pairs["g"], k, e, rows) * image
            ext.set(qb, k, e, rows, value)
            if k == 0 and FAR <= e < FAR + own:
                k0[own_rows(e - FAR, own, rows)] = value
    mixed, square = Sums(), Sums()
    for rows, e, tiles in ext.sweep(qb, FAR, FAR + own - 1):
        for k, (q, image) in enumerate(tiles):
            value = ext.at(pairs["g"], k, e, rows) * image
            (k1, k1_strip)[k][own_rows(e - FAR, own, rows)] = value
            ext.set(qa, k, e, rows, value)
            if k == 0:
                mixed.add(q * image)
                square.add(value * image)
    put_row(out, (mixed, square))
    for rows, e, tiles in ext.sweep(qa, FAR + NEAR - 1, FAR + own - NEAR):
        for k, (_, image) in enumerate(tiles):
            ext.set(qb, k, e, rows, ext.at(pairs["g"], k, e, rows) * image)
    for message, side in ((to_a, lon_even), (to_b, 1 - lon_even)):
        near, next_one = (jnp.where(side == 1, own - d, d - 1) for d in (1, NEAR))
        packed = jnp.zeros((levels, LANES), jnp.float32)
        for k, (main, strip) in enumerate(
            (
                (column(k1, near, own, levels), column(k1_strip, near, own, levels)),
                (column(k1, next_one, own, levels), column(k1_strip, next_one, own, levels)),
                [plane(ref, FAR + next_one, columns, levels)[...] for ref in qb],
            )
        ):
            message[k] = main
            rolled = turn(strip, 2 * GROUP * k + GROUP)
            packed = jnp.where(lane // (2 * GROUP) == k, rolled, packed)
        message[SECOND - 2] = packed
        message[SECOND - 1] = column(fd, near, own, levels)


def second_kernel(own, levels, columns, n_lat, k0, k1, k1_strip, from_a, from_b, g_main, g_strip, d_main, d_strip,
                  above, below, shift_sums, k2, k3, k4, out, shift_row, qa_main, qa_strip, qb_main, qb_strip, far):
    lon_even, _, _ = parity(n_lat)
    qa, qb = (qa_main, qa_strip), (qb_main, qb_strip)
    g = (g_main, g_strip)
    ext = Extended(columns, levels, (d_main, d_strip), g, above, below, far)
    for ref in (*qa, *qb):
        clear_ends(ref, columns, levels)
    row = total_row(shift_sums)
    mixed, square = lane_value(row, 0), lane_value(row, 1)
    shift = jnp.where(mixed > 0.0, square / jnp.where(mixed > 0.0, mixed, 1.0), 1.0)
    shift_row[...] = jnp.broadcast_to(shift, shift_row.shape)
    shift = jnp.broadcast_to(shift, (levels, LANES))
    for i in range(own):
        ext.put(qa, 0, FAR + i, column(k1, i, own, levels))
        ext.put(qa, 1, FAR + i, column(k1_strip, i, own, levels))
    for block, east in ((from_a, lon_even), (from_b, 1 - lon_even)):
        strips = [turn(block[SECOND - 2], -(2 * GROUP * k + GROUP)) for k in range(3)]
        near, next_one = (jnp.where(east == 1, FAR + own - 1 + d, FAR - d) for d in (1, NEAR))
        for k in range(2):
            first, other, image = ((block[d], strips[d])[k] for d in range(3))
            ext.put(qa, k, near, first)
            ext.put(qa, k, next_one, other)
            ext.put(qb, k, next_one, image - shift * other)
        far[east] = block[SECOND - 1]
    shift = shift[:SUBLANES]
    for rows, e, tiles in ext.sweep(qa, FAR - 1, FAR + own):
        for k, (q, image) in enumerate(tiles):
            value = ext.at(g, k, e, rows) * image - shift[: rows[1]] * q
            ext.set(qb, k, e, rows, value)
            if k == 0 and FAR <= e < FAR + own:
                k2[own_rows(e - FAR, own, rows)] = value
    for rows, e, tiles in ext.sweep(qb, FAR - 1, FAR + own):
        for k, (q, image) in enumerate(tiles):
            value = ext.at(g, k, e, rows) * image - shift[: rows[1]] * q
            ext.set(qa, k, e, rows, value)
            if k == 0 and FAR <= e < FAR + own:
                k3[own_rows(e - FAR, own, rows)] = value
    sums = [Sums() for _ in PAIRS]
    for rows, e, ((q, image),) in ext.sweep(qa, FAR, FAR + own - 1, strips=False):
        place = own_rows(e - FAR, own, rows)
        scale = ext.at(g, 0, e, rows)
        last = scale * image - shift[: rows[1]] * q
        k4[place] = last
        v = [k0[place], k1[place], k2[place], q, last]
        w = 1.0 / scale
        lead = [a * w for a in v]
        for total, (a, b) in zip(sums, PAIRS):
            total.add(lead[a] * v[b])
    put_row(out, sums)


def final_kernel(sums, shift_row, x, c, k0, k1, k2, k3, k4, out, rest):
    row = total_row(sums)
    first, *others = [lane_value(row, k) for k in range(len(PAIRS))]
    shift = lane_value(shift_row[...], 0)
    one = jnp.ones((1, 1), jnp.float32)
    solution, residual = krylov_coefficients(first, others[: 2 * ITERS], others[2 * ITERS :], shift, one)
    vectors = (k0, k1, k2, k3, k4)
    inverse = 1.0 / c[...]

    def combined(coefficients):
        total = None
        for a, v in zip(coefficients, vectors):
            term = a * v[...]
            total = term if total is None else total + term
        return total * inverse

    out[...] = x[...] + combined(solution)
    rest[...] = combined(residual)


def program(right_side, first_guess, cell_scale, helmholtz_term, vertical_coupling):
    n_lon, n_lat = lax.axis_size("lon"), lax.axis_size("lat")
    levels, own, width = right_side.shape
    assert width == LANES and own == 2 * NEAR >= FAR and len(FIELDS) * own * GROUP == LANES
    assert n_lon % 4 == 0 and n_lat % 2 == 0
    columns = own + 2 * FAR
    pairs = swap_pairs(n_lon, n_lat)
    coupling = vertical_coupling.reshape(1, levels - 1)
    b, x, c, h = (v.reshape(levels * own, LANES) for v in (right_side, first_guess, cell_scale, helmholtz_term))

    def real(*shape):
        return jax.ShapeDtypeStruct(shape, jnp.float32)

    def call(kernel, ins, outs, scratch=(), specs=None, aliases=()):
        return pl.pallas_call(
            kernel,
            out_shape=tuple(outs) if len(outs) > 1 else outs[0],
            in_specs=specs or [VMEM] * len(ins),
            out_specs=tuple([VMEM] * len(outs)) if len(outs) > 1 else VMEM,
            scratch_shapes=[pltpu.VMEM(s, jnp.float32) if isinstance(s, tuple) else s for s in scratch],
            compiler_params=pltpu.CompilerParams(vmem_limit_bytes=32 * 1024 * 1024),
            input_output_aliases=dict(aliases),
        )(*ins)

    def swap(value, name):
        return lax.ppermute(value, AXES, pairs[name])

    def everywhere(rows):
        return lax.all_to_all(rows, AXES, 0, 0, tiled=True)

    whole = real(levels * own, LANES)
    tile = real(levels, LANES)
    rows = real(n_lon * n_lat, 1, LANES)
    extended = ((levels + 2) * columns, LANES)

    to_a, to_b, lat_a, lat_b, above, below, *fields = call(
        functools.partial(pack_kernel, own, levels, n_lat),
        tuple(pltpu.with_memory_space_constraint(v, pltpu.HBM) for v in (x, b, c, h, coupling)),
        [real(len(FIRST), levels, LANES)] * 2 + [tile] * 4 + [whole] * len(FIELDS),
        [(levels * own, LANES)] * 4
        + [(1, levels - 1), ((levels + 2) * own, LANES), (2, levels, LANES), pltpu.SemaphoreType.DMA((5,))],
        [pl.BlockSpec(memory_space=pltpu.HBM)] * 5,
    )
    lat_a = swap(lat_a, "lat_even")
    lat_b = swap(lat_b, "lat_odd")
    from_a = swap(to_a, "lon_even")
    from_b = swap(to_b, "lon_odd")
    corners_a, corners_b = call(
        functools.partial(corner_kernel, own, levels, n_lat), (lat_a, lat_b), [tile] * 2
    )
    corners_a = swap(corners_a, "lon_even")
    corners_b = swap(corners_b, "lon_odd")
    buffers = call(
        functools.partial(own_kernel, own, levels, columns, n_lat),
        (*fields, lat_a, lat_b),
        [real(*extended)] * 2 * len(FIELDS),
    )
    ins = (fields[2], above, below, from_a, from_b, corners_a, corners_b, *buffers)
    *buffers, k0, k1, k1_strip, to_a, to_b, shift_sums = call(
        functools.partial(first_kernel, own, levels, columns, n_lat),
        ins,
        [real(*extended)] * 2 * len(FIELDS)
        + [whole] * 3
        + [real(SECOND, levels, LANES)] * 2
        + [rows],
        [extended] * 2,
        aliases=[(len(ins) - 2 * len(FIELDS) + k, k) for k in range(2 * len(FIELDS))],
    )
    coefficients = buffers[2:6]
    from_a = swap(to_a, "lon_even")
    from_b = swap(to_b, "lon_odd")
    shift_sums = everywhere(shift_sums)
    k2, k3, k4, sums, shift = call(
        functools.partial(second_kernel, own, levels, columns, n_lat),
        (k0, k1, k1_strip, from_a, from_b, *coefficients, above, below, shift_sums),
        [whole] * 3 + [rows, real(1, LANES)],
        [extended] * 4 + [(2, levels, LANES)],
    )
    sums = everywhere(sums)
    out, rest = call(final_kernel, (sums, shift, x, c, k0, k1, k2, k3, k4), [whole] * 2)
    return out.reshape(right_side.shape), rest.reshape(right_side.shape)


def solution(mesh):
    spec = P(None, "lon", "lat")
    return jax.shard_map(
        program, mesh=mesh, in_specs=(spec, spec, spec, spec, P()), out_specs=(spec, spec), check_vma=False
    )
```

```python
import functools

import jax
import jax.numpy as jnp
from jax import lax
from jax.experimental import pallas as pl
from jax.experimental.pallas import tpu as pltpu
from jax.sharding import PartitionSpec as P


AXES = ("lon", "lat")
ITERS = 2
LANES = 128
SUBLANES = 8
NEAR, FAR = 2, 3
GROUP = 8
VMEM = pl.BlockSpec(memory_space=pltpu.VMEM)
FIRST = ("q", "s", "g")
STRIPS = (("q", 1), ("q", 2), ("g", 1), ("d", 1), ("s", 1))
SECOND = 5
FIELDS = ("q", "g", "d", "s")


def swap_pairs(n_lon, n_lat):
    half = n_lon // 2

    def flat(move):
        pairs = []
        for i in range(n_lon):
            for j in range(n_lat):
                k, m = move(i, j)
                pairs.append((i * n_lat + j, k * n_lat + m))
        return pairs

    def lat_odd(i, j):
        if j == 0 or j == n_lat - 1:
            return (i + half) % n_lon, j
        return i, ((j + 1) ^ 1) - 1

    return {
        "lon_even": flat(lambda i, j: (i ^ 1, j)),
        "lon_odd": flat(lambda i, j: ((((i + 1) ^ 1) - 1) % n_lon, j)),
        "lat_even": flat(lambda i, j: (i, j ^ 1)),
        "lat_odd": flat(lat_odd),
    }


def plus(a, b):
    if a is None or b is None:
        return b if a is None else a
    return a + b


def times(a, b):
    return None if a is None or b is None else a * b


def add_scaled(a, scale, b):
    size = max(len(a), len(b))
    a, b = (list(v) + [None] * (size - len(v)) for v in (a, b))
    return [plus(x, times(scale, y)) for x, y in zip(a, b)]


def krylov_coefficients(first, mixed, rest, shift, one):
    def inner(a, b):
        total = times(times(a[0], b[0]), first)
        for x, others in ((a[0], b), (b[0], a)):
            for j in range(1, len(others)):
                total = plus(total, times(times(x, others[j]), mixed[j - 1]))
        for k in range(len(a) + len(b) - 3):
            part = None
            for i in range(1, len(a)):
                if 1 <= k + 2 - i < len(b):
                    part = plus(part, times(a[i], b[k + 2 - i]))
            total = plus(total, times(part, rest[k]))
        return total

    def image_of(a):
        return [None] + [plus(v, times(shift, a[k + 1]) if k + 1 < len(a) else None) for k, v in enumerate(a)]

    shadow = [one]
    residual = [one]
    direction = [one]
    solution = []
    rho = first
    for iteration in range(ITERS):
        image = image_of(direction)
        alpha = rho / inner(shadow, image)
        half = add_scaled(residual, -alpha, image)
        second = image_of(half)
        omega = inner(second, half) / inner(second, second)
        solution = add_scaled(solution, alpha, direction)
        solution = add_scaled(solution, omega, half)
        residual = add_scaled(half, -omega, second)
        if iteration + 1 < ITERS:
            rho_next = inner(shadow, half) - omega * inner(shadow, second)
            beta = rho_next / rho * (alpha / omega)
            direction = add_scaled(residual, beta, add_scaled(direction, -omega, image))
            rho = rho_next
    return solution, residual


PAIRS = (
    [(0, j) for j in range(2 * ITERS + 1)]
    + [(1 + k // 2, 1 + k - k // 2) for k in range(4 * ITERS - 1)]
)


def lanes_of(levels):
    return lax.broadcasted_iota(jnp.int32, (levels, LANES), 1)


def turn(value, shift):
    shift %= LANES
    return value if shift == 0 else pltpu.roll(value, shift, 1)


def plane(ref, column, columns, levels, shift=0):
    return ref.at[pl.ds((1 + shift) * columns + column, levels, stride=columns), :]


def clear_ends(ref, columns, levels):
    ref[0:columns, :] = jnp.zeros((columns, LANES), jnp.float32)
    ref[(levels + 1) * columns : (levels + 2) * columns, :] = jnp.zeros((columns, LANES), jnp.float32)


def column(ref, i, own, levels):
    return ref[pl.ds(i, levels, stride=own), :]


def shifted_rows(main, strip, lane, strips=True):
    main_s, main_n = turn(main, -1), turn(main, 1)
    strip_s, strip_n = turn(strip, -1), turn(strip, 1)
    first, last = lane == 0, lane == LANES - 1
    out = [jnp.where(last, strip_s, main_s) + jnp.where(first, strip_n, main_n)]
    if strips:
        out.append(jnp.where(last, main_s, strip_s) + jnp.where(first, main_n, strip_n))
    return out


def transformed(x, b, c, h, above, below):
    return {"q": c * x, "g": c * c, "d": (4.0 + h) + (above + below), "s": c * b}


def parity(size):
    i, j = lax.axis_index("lon"), lax.axis_index("lat")
    pole = (j == 0) | (j == size - 1)
    return 1 - lax.rem(i, 2), 1 - lax.rem(j, 2), pole


def pack_kernel(own, levels, n_lat, x_hbm, b_hbm, c_hbm, h_hbm, coupling_hbm, to_a, to_b, lat_a, lat_b, above,
                below, fq, fg, fd, fs, x, b, c, h, coupling, q_ref, partial, sem):
    copies = []
    moves = ((coupling_hbm, coupling), (x_hbm, x), (c_hbm, c), (h_hbm, h), (b_hbm, b))
    for k, (source, target) in enumerate(moves):
        copies.append(pltpu.make_async_copy(source, target, sem.at[k]))
        copies[-1].start()
    lane = lanes_of(levels)
    groups = LANES // GROUP
    lon_even, lat_even, pole = parity(n_lat)
    store = dict(zip(FIELDS, (fq, fg, fd, fs)))
    copies[0].wait()
    wide = (levels, levels - 1)
    row, interface = (lax.broadcasted_iota(jnp.int32, wide, k) for k in (0, 1))
    strength = jnp.broadcast_to(coupling[...], wide)
    for out, k in ((below, row), (above, row - 1)):
        value = jnp.sum(jnp.where(interface == k, strength, 0.0), axis=1, keepdims=True)
        out[...] = jnp.broadcast_to(value, (levels, LANES))
    for copy in copies[1:]:
        copy.wait()
    for start in range(0, levels, SUBLANES):
        rows = start, min(SUBLANES, levels - start)
        block, shape = slice(start, start + rows[1]), (rows[1], LANES)
        row_lane = lanes_of(rows[1])
        group = row_lane // GROUP
        north = jnp.zeros(shape, jnp.float32)
        south = north
        for i in range(own):
            place = own_rows(i, own, rows)
            values = transformed(x[place], b[place], c[place], h[place], above[block, :], below[block, :])
            for f, name in enumerate(FIELDS):
                store[name][place] = values[name]
                if name == "q":
                    q_ref[pl.ds((1 + start) * own + i, rows[1], stride=own), :] = values[name]
                slot = f * own + i
                rolled = turn(values[name], GROUP * slot)
                north = jnp.where(group == slot, rolled, north)
                south = jnp.where(group == (slot - 1) % groups, rolled, south)
        even = jnp.full(shape, lat_even, jnp.int32) == 1
        over = jnp.full(shape, pole.astype(jnp.int32), jnp.int32) == 1
        lat_a[block, :] = jnp.where(even, south, north)
        other = jnp.where(even, north, south)
        mirror = other
        for bit in (1, 2, 4):
            mirror = jnp.where((row_lane & bit) != 0, turn(mirror, bit), turn(mirror, -bit))
        mirror = jnp.where(even, turn(mirror, -GROUP), turn(mirror, GROUP))
        lat_b[block, :] = jnp.where(over, mirror, other)
    clear_ends(q_ref, own, levels)
    for k, (i, inner) in enumerate(((0, 1), (own - 1, own - 2))):
        q = plane(q_ref, i, own, levels)[...]
        near = jnp.where(lane == LANES - 1, 0.0, turn(q, -1)) + jnp.where(lane == 0, 0.0, turn(q, 1))
        near = near + plane(q_ref, inner, own, levels)[...]
        near = near + below[...] * plane(q_ref, i, own, levels, 1)[...]
        near = near + above[...] * plane(q_ref, i, own, levels, -1)[...]
        image = column(fd, i, own, levels) * q - near
        partial[k] = column(fs, i, own, levels) - column(fg, i, own, levels) * image
    for message, side in ((to_a, lon_even), (to_b, 1 - lon_even)):
        i = jnp.where(side == 1, own - 1, 0)
        message[0] = column(fq, i, own, levels)
        message[1] = partial[side]
        message[2] = column(fg, i, own, levels)


def corner_kernel(own, levels, n_lat, lat_a, lat_b, to_a, to_b):
    lane = lanes_of(levels)
    quarter = (lane // GROUP) % own
    lon_even, lat_even, _ = parity(n_lat)
    even = jnp.full((levels, LANES), lat_even, jnp.int32) == 1
    lon = jnp.full((levels, LANES), lon_even, jnp.int32) == 1
    a, b = lat_a[...], lat_b[...]
    north, south = jnp.where(even, b, a), jnp.where(even, a, b)
    east = jnp.where(quarter >= own - NEAR, south, turn(north, GROUP * (1 - NEAR)))
    west = jnp.where(quarter < NEAR, south, turn(north, GROUP * (1 + NEAR)))
    to_a[...] = jnp.where(lon, east, west)
    to_b[...] = jnp.where(lon, west, east)


def lane_value(row, k):
    lane = lax.broadcasted_iota(jnp.int32, (1, LANES), 1)
    return jnp.sum(jnp.where(lane == k, row, 0.0), axis=1, keepdims=True)


def put_row(out, arrays):
    lane = lax.broadcasted_iota(jnp.int32, (1, LANES), 1)
    row = jnp.zeros((1, LANES), jnp.float32)
    for k, value in enumerate(arrays):
        row = jnp.where(lane == k, value.total(), row)
    out[...] = jnp.broadcast_to(row[None], out.shape)


def total_row(gathered):
    return jnp.sum(gathered[...], axis=0)


class Extended:
    def __init__(self, columns, levels, d, g, above, below, far=None):
        self.columns, self.levels = columns, levels
        self.d, self.g = d, g
        self.above, self.below = above, below
        self.far = far

    def at(self, pair, k, e, rows, shift=0):
        start, count = rows
        return pair[k][pl.ds((1 + start + shift) * self.columns + e, count, stride=self.columns), :]

    def set(self, pair, k, e, rows, value):
        start, count = rows
        pair[k][pl.ds((1 + start) * self.columns + e, count, stride=self.columns), :] = value

    def put(self, pair, k, e, value):
        self.set(pair, k, e, (0, self.levels), value)

    def diagonal(self, k, e, rows):
        edges = (FAR - 1, self.columns - FAR)
        if self.far is not None and k == 0 and e in edges:
            start, count = rows
            return self.far[edges.index(e), start : start + count, :]
        return self.at(self.d, k, e, rows)

    def sweep(self, pair, first, last, strips=True):
        for start in range(0, self.levels, SUBLANES):
            rows = start, min(SUBLANES, self.levels - start)
            lane = lanes_of(rows[1])
            above, below = (ref[start : start + rows[1], :] for ref in (self.above, self.below))
            center = {}

            def middle(k, e):
                if (k, e) not in center:
                    center[k, e] = self.at(pair, k, e, rows)
                return center[k, e]

            for e in range(first, last + 1):
                near = shifted_rows(middle(0, e), middle(1, e), lane, strips)
                out = []
                for k in range(1 + strips):
                    q = middle(k, e)
                    side = middle(k, e - 1) + middle(k, e + 1)
                    levels = below * self.at(pair, k, e, rows, 1) + above * self.at(pair, k, e, rows, -1)
                    out.append((q, self.diagonal(k, e, rows) * q - (side + near[k]) - levels))
                yield rows, e, out


class Sums:
    def __init__(self):
        self.parts = {}

    def add(self, value):
        count = value.shape[0]
        self.parts[count] = self.parts[count] + value if count in self.parts else value

    def total(self):
        return sum(jnp.sum(v, keepdims=True) for v in self.parts.values())


def own_rows(i, own, rows):
    start, count = rows
    return pl.ds(start * own + i, count, stride=own), slice(None)


def own_kernel(own, levels, columns, n_lat, fq, fg, fd, fs, lat_a, lat_b, *outs):
    group = lanes_of(levels) // GROUP
    _, lat_even, _ = parity(n_lat)
    even = jnp.full((levels, LANES), lat_even, jnp.int32) == 1
    a, b = lat_a[...], lat_b[...]
    north, south = jnp.where(even, b, a), jnp.where(even, a, b)
    for f, field in enumerate((fq, fg, fd, fs)):
        main, strip = outs[2 * f : 2 * f + 2]
        if f == 0:
            clear_ends(main, columns, levels)
            clear_ends(strip, columns, levels)
        for i in range(own):
            slot = f * own + i
            plane(main, FAR + i, columns, levels)[...] = column(field, i, own, levels)
            edges = turn(jnp.where(group == slot, south, north), -GROUP * slot)
            plane(strip, FAR + i, columns, levels)[...] = edges


def first_kernel(own, levels, columns, n_lat, fd, above, below, from_a, from_b, corners_a, corners_b, *refs):
    extended = refs[8:16]
    k0, k1, k1_strip, to_a, to_b, out, qb_main, qb_strip = refs[16:]
    lane = lanes_of(levels)
    low = lane < LANES // 2
    lon_even, _, _ = parity(n_lat)
    pairs = {name: extended[2 * f : 2 * f + 2] for f, name in enumerate(FIELDS)}
    qa, qb = pairs["q"], (qb_main, qb_strip)
    ext = Extended(columns, levels, pairs["d"], pairs["g"], above, below)
    for ref in qb:
        clear_ends(ref, columns, levels)
    for block, corner, east in ((from_a, corners_a, lon_even), (from_b, corners_b, 1 - lon_even)):
        tile = corner[...]
        for k, name in enumerate(FIRST):
            ext.put(pairs[name], 0, jnp.where(east == 1, FAR + own, FAR - 1), block[k])
        for name, distance in STRIPS:
            e = jnp.where(east == 1, FAR + own - 1 + distance, FAR - distance)
            slot = FIELDS.index(name) * own + jnp.where(east == 1, distance - 1, own - distance)
            south = lax.rem(2 * LANES - GROUP * slot, LANES)
            north = lax.rem(south + LANES - GROUP * jnp.where(east == 1, 1 + NEAR, 1 - NEAR), LANES)
            ext.put(pairs[name], 1, e, jnp.where(low, pltpu.roll(tile, south, 1), pltpu.roll(tile, north, 1)))
    edges = {FAR - 1: FAR, FAR + own: FAR + own - 1}
    for rows, e, tiles in ext.sweep(qa, FAR - 1, FAR + own):
        for k, (_, image) in enumerate(tiles):
            if k == 0 and e in edges:
                edge, strip = ext.at(qa, 0, edges[e], rows), ext.at(qa, 1, e, rows)
                place = lanes_of(rows[1])
                beyond = jnp.where(place == LANES - 1, turn(strip, -1), 0.0) + jnp.where(
                    place == 0, turn(strip, 1), 0.0
                )
                image = -(edge + beyond)
            value = ext.at(pairs["s"], k, e, rows) - ext.at(pairs["g"], k, e, rows) * image
            ext.set(qb, k, e, rows, value)
            if k == 0 and FAR <= e < FAR + own:
                k0[own_rows(e - FAR, own, rows)] = value
    mixed, square = Sums(), Sums()
    for rows, e, tiles in ext.sweep(qb, FAR, FAR + own - 1):
        for k, (q, image) in enumerate(tiles):
            value = ext.at(pairs["g"], k, e, rows) * image
            (k1, k1_strip)[k][own_rows(e - FAR, own, rows)] = value
            ext.set(qa, k, e, rows, value)
            if k == 0:
                mixed.add(q * image)
                square.add(value * image)
    put_row(out, (mixed, square))
    for rows, e, tiles in ext.sweep(qa, FAR + NEAR - 1, FAR + own - NEAR):
        for k, (_, image) in enumerate(tiles):
            ext.set(qb, k, e, rows, ext.at(pairs["g"], k, e, rows) * image)
    for message, side in ((to_a, lon_even), (to_b, 1 - lon_even)):
        near, next_one = (jnp.where(side == 1, own - d, d - 1) for d in (1, NEAR))
        packed = jnp.zeros((levels, LANES), jnp.float32)
        for k, (main, strip) in enumerate(
            (
                (column(k1, near, own, levels), column(k1_strip, near, own, levels)),
                (column(k1, next_one, own, levels), column(k1_strip, next_one, own, levels)),
                [plane(ref, FAR + next_one, columns, levels)[...] for ref in qb],
            )
        ):
            message[k] = main
            rolled = turn(strip, 2 * GROUP * k + GROUP)
            packed = jnp.where(lane // (2 * GROUP) == k, rolled, packed)
        message[SECOND - 2] = packed
        message[SECOND - 1] = column(fd, near, own, levels)


def second_kernel(own, levels, columns, n_lat, k0, k1, k1_strip, from_a, from_b, g_main, g_strip, d_main, d_strip,
                  above, below, shift_sums, k2, k3, k4, out, shift_row, qa_main, qa_strip, qb_main, qb_strip, far):
    lon_even, _, _ = parity(n_lat)
    qa, qb = (qa_main, qa_strip), (qb_main, qb_strip)
    g = (g_main, g_strip)
    ext = Extended(columns, levels, (d_main, d_strip), g, above, below, far)
    for ref in (*qa, *qb):
        clear_ends(ref, columns, levels)
    row = total_row(shift_sums)
    mixed, square = lane_value(row, 0), lane_value(row, 1)
    shift = jnp.where(mixed > 0.0, square / jnp.where(mixed > 0.0, mixed, 1.0), 1.0)
    shift_row[...] = jnp.broadcast_to(shift, shift_row.shape)
    shift = jnp.broadcast_to(shift, (levels, LANES))
    for i in range(own):
        ext.put(qa, 0, FAR + i, column(k1, i, own, levels))
        ext.put(qa, 1, FAR + i, column(k1_strip, i, own, levels))
    for block, east in ((from_a, lon_even), (from_b, 1 - lon_even)):
        strips = [turn(block[SECOND - 2], -(2 * GROUP * k + GROUP)) for k in range(3)]
        near, next_one = (jnp.where(east == 1, FAR + own - 1 + d, FAR - d) for d in (1, NEAR))
        for k in range(2):
            first, other, image = ((block[d], strips[d])[k] for d in range(3))
            ext.put(qa, k, near, first)
            ext.put(qa, k, next_one, other)
            ext.put(qb, k, next_one, image - shift * other)
        far[east] = block[SECOND - 1]
    shift = shift[:SUBLANES]
    for rows, e, tiles in ext.sweep(qa, FAR - 1, FAR + own):
        for k, (q, image) in enumerate(tiles):
            value = ext.at(g, k, e, rows) * image - shift[: rows[1]] * q
            ext.set(qb, k, e, rows, value)
            if k == 0 and FAR <= e < FAR + own:
                k2[own_rows(e - FAR, own, rows)] = value
    for rows, e, tiles in ext.sweep(qb, FAR - 1, FAR + own):
        for k, (q, image) in enumerate(tiles):
            value = ext.at(g, k, e, rows) * image - shift[: rows[1]] * q
            ext.set(qa, k, e, rows, value)
            if k == 0 and FAR <= e < FAR + own:
                k3[own_rows(e - FAR, own, rows)] = value
    sums = [Sums() for _ in PAIRS]
    for rows, e, ((q, image),) in ext.sweep(qa, FAR, FAR + own - 1, strips=False):
        place = own_rows(e - FAR, own, rows)
        scale = ext.at(g, 0, e, rows)
        last = scale * image - shift[: rows[1]] * q
        k4[place] = last
        v = [k0[place], k1[place], k2[place], q, last]
        w = 1.0 / scale
        lead = [a * w for a in v]
        for total, (a, b) in zip(sums, PAIRS):
            total.add(lead[a] * v[b])
    put_row(out, sums)


def final_kernel(sums, shift_row, x, c, k0, k1, k2, k3, k4, out, rest):
    row = total_row(sums)
    first, *others = [lane_value(row, k) for k in range(len(PAIRS))]
    shift = lane_value(shift_row[...], 0)
    one = jnp.ones((1, 1), jnp.float32)
    solution, residual = krylov_coefficients(first, others[: 2 * ITERS], others[2 * ITERS :], shift, one)
    vectors = (k0, k1, k2, k3, k4)
    solution, residual = ([jnp.broadcast_to(a, (SUBLANES, LANES)) for a in v] for v in (solution, residual))
    size = x.shape[0]
    for start in range(0, size, SUBLANES):
        count = min(SUBLANES, size - start)
        block = slice(start, start + count)
        inverse = 1.0 / c[block, :]
        values = [v[block, :] for v in vectors]

        def combined(coefficients):
            total = None
            for a, v in zip(coefficients, values):
                term = a[:count] * v
                total = term if total is None else total + term
            return total * inverse

        out[block, :] = x[block, :] + combined(solution)
        rest[block, :] = combined(residual)


def program(right_side, first_guess, cell_scale, helmholtz_term, vertical_coupling):
    n_lon, n_lat = lax.axis_size("lon"), lax.axis_size("lat")
    levels, own, width = right_side.shape
    assert width == LANES and own == 2 * NEAR >= FAR and len(FIELDS) * own * GROUP == LANES
    assert n_lon % 4 == 0 and n_lat % 2 == 0
    columns = own + 2 * FAR
    pairs = swap_pairs(n_lon, n_lat)
    coupling = vertical_coupling.reshape(1, levels - 1)
    b, x, c, h = (v.reshape(levels * own, LANES) for v in (right_side, first_guess, cell_scale, helmholtz_term))

    def real(*shape):
        return jax.ShapeDtypeStruct(shape, jnp.float32)

    def call(kernel, ins, outs, scratch=(), specs=None, aliases=()):
        return pl.pallas_call(
            kernel,
            out_shape=tuple(outs) if len(outs) > 1 else outs[0],
            in_specs=specs or [VMEM] * len(ins),
            out_specs=tuple([VMEM] * len(outs)) if len(outs) > 1 else VMEM,
            scratch_shapes=[pltpu.VMEM(s, jnp.float32) if isinstance(s, tuple) else s for s in scratch],
            compiler_params=pltpu.CompilerParams(vmem_limit_bytes=32 * 1024 * 1024),
            input_output_aliases=dict(aliases),
        )(*ins)

    def swap(value, name):
        return lax.ppermute(value, AXES, pairs[name])

    def everywhere(rows):
        return lax.all_to_all(rows, AXES, 0, 0, tiled=True)

    whole = real(levels * own, LANES)
    tile = real(levels, LANES)
    rows = real(n_lon * n_lat, 1, LANES)
    extended = ((levels + 2) * columns, LANES)

    to_a, to_b, lat_a, lat_b, above, below, *fields = call(
        functools.partial(pack_kernel, own, levels, n_lat),
        tuple(pltpu.with_memory_space_constraint(v, pltpu.HBM) for v in (x, b, c, h, coupling)),
        [real(len(FIRST), levels, LANES)] * 2 + [tile] * 4 + [whole] * len(FIELDS),
        [(levels * own, LANES)] * 4
        + [(1, levels - 1), ((levels + 2) * own, LANES), (2, levels, LANES), pltpu.SemaphoreType.DMA((5,))],
        [pl.BlockSpec(memory_space=pltpu.HBM)] * 5,
    )
    lat_a = swap(lat_a, "lat_even")
    lat_b = swap(lat_b, "lat_odd")
    from_a = swap(to_a, "lon_even")
    from_b = swap(to_b, "lon_odd")
    corners_a, corners_b = call(
        functools.partial(corner_kernel, own, levels, n_lat), (lat_a, lat_b), [tile] * 2
    )
    corners_a = swap(corners_a, "lon_even")
    corners_b = swap(corners_b, "lon_odd")
    buffers = call(
        functools.partial(own_kernel, own, levels, columns, n_lat),
        (*fields, lat_a, lat_b),
        [real(*extended)] * 2 * len(FIELDS),
    )
    ins = (fields[2], above, below, from_a, from_b, corners_a, corners_b, *buffers)
    *buffers, k0, k1, k1_strip, to_a, to_b, shift_sums = call(
        functools.partial(first_kernel, own, levels, columns, n_lat),
        ins,
        [real(*extended)] * 2 * len(FIELDS)
        + [whole] * 3
        + [real(SECOND, levels, LANES)] * 2
        + [rows],
        [extended] * 2,
        aliases=[(len(ins) - 2 * len(FIELDS) + k, k) for k in range(2 * len(FIELDS))],
    )
    coefficients = buffers[2:6]
    from_a = swap(to_a, "lon_even")
    from_b = swap(to_b, "lon_odd")
    shift_sums = everywhere(shift_sums)
    k2, k3, k4, sums, shift = call(
        functools.partial(second_kernel, own, levels, columns, n_lat),
        (k0, k1, k1_strip, from_a, from_b, *coefficients, above, below, shift_sums),
        [whole] * 3 + [rows, real(1, LANES)],
        [extended] * 4 + [(2, levels, LANES)],
    )
    sums = everywhere(sums)
    out, rest = call(final_kernel, (sums, shift, x, c, k0, k1, k2, k3, k4), [whole] * 2)
    return out.reshape(right_side.shape), rest.reshape(right_side.shape)


def solution(mesh):
    spec = P(None, "lon", "lat")
    return jax.shard_map(
        program, mesh=mesh, in_specs=(spec, spec, spec, spec, P()), out_specs=(spec, spec), check_vma=False
    )
```
